128 devices in a mesh: dp: 16 (over x, y_lo, core), mp: 8 (over z, y_hi).
Axes of the slice: x: 4, y: 4 (y_hi: 2, y_lo: 2; y = y_hi * 2 + y_lo), z: 4, core: 2. Of those that a mesh axis runs over, the one named last changes fastest.
Arguments:
- tokens: bfloat16 [4096, 32768], P('dp', 'mp'), may hold values from -6 to 6
- block_weights: bfloat16 [128, 8, 256, 256], P('mp'), may hold values from -0.125 to 0.125
- lowrank_down: bfloat16 [32768, 256], P(('mp', 'dp')), may hold values from -0.03125 to 0.03125
- lowrank_up: bfloat16 [32768, 256], P(('mp', 'dp')), may hold values from -0.375 to 0.375
- cotangent: bfloat16 [4096, 32768], P('dp', 'mp'), may hold values from -6 to 6
- seq_lengths: int32 [16], P('dp'), may hold values from 64 to 256, as said below
Outputs:
- output: bfloat16 [4096, 32768], P('dp', 'mp')
- grad_tokens: bfloat16 [4096, 32768], P('dp', 'mp')
- grad_blocks: bfloat16 [128, 8, 256, 256], P(('mp', 'dp'))
- grad_lowrank: bfloat16 [32768, 2, 256], P(('mp', 'dp'))
The draws below stay inside these ranges and needn't reach their ends.
Inputs may be any that keep to these rules, and one draw needn't show every extreme that they name: `seq_lengths`: each data shard holds one sequence in 256 slots, live from the first slot; some shard is full and some shard holds exactly 64 live tokens.
All inputs are finite; a program needn't handle non-finite values.
Results may differ from the reference program's by a relative error of at most 0.025.
Values may be sent and summed in bfloat16 or wider, within the bound.
No kernel may reach another device: no remote copies, remote signals or barrier semaphores. Data moves between devices by JAX's collectives and lax.ppermute only.
A program may use at most 192 MiB of HBM per device.

```python
import jax
import jax.numpy as jnp
import numpy as np
from jax import lax

W = 32768
BLOCK = 256
LEVELS = 8
RANK = 256
TOK_DEV = 256
TOKENS = 4096
BLOCKS = 128
N_DP = 16


def draw_seq_lengths(key, part):
    first_key, second_key = jax.random.split(jax.random.fold_in(key, 7))
    lengths = jax.random.randint(first_key, (N_DP,), TOK_DEV // 4, TOK_DEV + 1)
    order = jax.random.permutation(second_key, N_DP)
    lengths = lengths.at[order[0]].set(TOK_DEV)
    lengths = lengths.at[order[1]].set(TOK_DEV // 4)
    return lengths.astype(jnp.int32)


def level_of(key, dims, cuts, smallest, high):
    level = 1.0
    for dim, blocks in cuts:
        heights = jax.random.uniform(jax.random.fold_in(jax.random.fold_in(key, 6), dim), (blocks,), jnp.float32, smallest / len(cuts), high / len(cuts))
        level = level * jnp.repeat(jnp.exp(heights), dims[dim] // blocks).reshape((-1,) + (1,) * (len(dims) - 1 - dim))
    return level


def noise(own_key, extent, deviation, limit, cuts=(), kind=jnp.bfloat16):
    drawn = deviation * jax.random.normal(own_key, extent, jnp.float32)
    if cuts:
        drawn = drawn * level_of(own_key, extent, cuts, -0.22, 0.18)
    return jnp.clip(drawn, -limit, limit).astype(kind)


def setup_inputs(seed: int = 0) -> dict:
    arg_keys = jax.random.split(jax.random.key(seed), 7)
    return {
        "tokens": noise(arg_keys[0], (TOKENS, W), 1.0, 6.0, ((0, 16), (1, 8))),
        "block_weights": noise(arg_keys[1], (BLOCKS, LEVELS, BLOCK, BLOCK), (LEVELS * BLOCK) ** -0.5, 0.125, ((0, 8),)),
        "lowrank_down": noise(arg_keys[2], (W, RANK), W ** -0.5, 0.03125, ((0, 128),)),
        "lowrank_up": noise(arg_keys[3], (W, RANK), RANK ** -0.5, 0.375, ((0, 128),)),
        "cotangent": noise(arg_keys[4], (TOKENS, W), 1.0, 6.0, ((0, 16), (1, 8))),
        "seq_lengths": draw_seq_lengths(jax.random.fold_in(arg_keys[6], 71), 0),
    }


def activate(values):
    return jax.nn.gelu(values, approximate=True)

def reference(tokens, block_weights, lowrank_down, lowrank_up, cotangent, seq_lengths):
    block_count = W // BLOCK
    table_np = np.array([[index if level == 0 else index ^ 1 << level - 1 for level in range(LEVELS)] for index in range(block_count)], dtype=np.int32)
    table = jnp.asarray(table_np)
    slot_ids = jnp.arange(TOKENS, dtype=jnp.int32)
    position = slot_ids % TOK_DEV
    shard_ids = slot_ids // TOK_DEV
    live = (position < seq_lengths[shard_ids]).astype(jnp.float32)[:, None]
    tok_blocks = tokens.reshape(TOKENS, block_count, BLOCK)
    down_proj = jnp.dot(tokens, lowrank_down, preferred_element_type=jnp.float32).astype(jnp.bfloat16)
    block_iota = jnp.arange(block_count, dtype=jnp.int32)
    level_iota = jnp.arange(LEVELS, dtype=jnp.int32)

    def forward_block(index):
        gathered = jnp.take(tok_blocks, table[index], axis=1).reshape(TOKENS, LEVELS * BLOCK)
        return jnp.dot(gathered, block_weights[index].reshape(LEVELS * BLOCK, BLOCK), preferred_element_type=jnp.float32)
    butterfly = lax.map(forward_block, block_iota)
    hidden = jnp.transpose(butterfly, (1, 0, 2)).reshape(TOKENS, W)
    hidden = hidden + jnp.dot(down_proj, lowrank_up.T, preferred_element_type=jnp.float32)
    output = (live * activate(hidden)).astype(jnp.bfloat16)
    _, pullback = jax.vjp(activate, hidden)
    pre_grad, = pullback(live * cotangent.astype(jnp.float32))
    grad_hidden = pre_grad.astype(jnp.bfloat16)
    up_proj = jnp.dot(grad_hidden, lowrank_up, preferred_element_type=jnp.float32).astype(jnp.bfloat16)
    hid_blocks = grad_hidden.reshape(TOKENS, block_count, BLOCK)

    def backward_block(index):
        sources = table[index]
        incoming = jnp.take(hid_blocks, sources, axis=1).astype(jnp.float32)
        matrices = block_weights[sources, level_iota].astype(jnp.float32)
        terms = jnp.einsum('tld,lcd->tlc', incoming, matrices).astype(jnp.bfloat16)
        terms = lax.optimization_barrier(terms)
        return lax.optimization_barrier(jnp.sum(terms.astype(jnp.float32), axis=1))
    back = lax.map(backward_block, block_iota)
    grad_tokens = jnp.transpose(back, (1, 0, 2)).reshape(TOKENS, W)
    grad_tokens = (grad_tokens + jnp.dot(up_proj, lowrank_down.T, preferred_element_type=jnp.float32)).astype(jnp.bfloat16)

    def weight_block(index):
        gathered = jnp.take(tok_blocks, table[index], axis=1).reshape(N_DP, TOK_DEV, LEVELS * BLOCK).astype(jnp.float32)
        hid_part = hid_blocks[:, index].reshape(N_DP, TOK_DEV, BLOCK).astype(jnp.float32)
        shard_grad = jnp.einsum('stc,std->scd', gathered, hid_part).astype(jnp.bfloat16)
        shard_grad = lax.optimization_barrier(shard_grad)
        return lax.optimization_barrier(jnp.sum(shard_grad.astype(jnp.float32), axis=0)).astype(jnp.bfloat16).reshape(LEVELS, BLOCK, BLOCK)
    grad_blocks = lax.map(weight_block, block_iota)

    def factor_shard(carry, pieces):
        tok_part, hid_part, down_part, up_part = pieces
        grad_down = jnp.dot(tok_part.T, up_part, preferred_element_type=jnp.float32)
        grad_up = jnp.dot(hid_part.T, down_part, preferred_element_type=jnp.float32)
        shard_factor = jnp.stack([grad_down, grad_up], axis=1).astype(jnp.bfloat16)
        shard_factor = lax.optimization_barrier(shard_factor)
        return (carry + shard_factor.astype(jnp.float32), None)
    initial = jnp.zeros((W, 2, RANK), jnp.float32)
    pieces = (tokens.reshape(N_DP, TOK_DEV, W), grad_hidden.reshape(N_DP, TOK_DEV, W), down_proj.reshape(N_DP, TOK_DEV, RANK), up_proj.reshape(N_DP, TOK_DEV, RANK))
    summed, _ = lax.scan(factor_shard, initial, pieces)
    grad_lowrank = summed.astype(jnp.bfloat16)
    return (output, grad_tokens, grad_blocks, grad_lowrank)
```

```python
import functools

import jax
import jax.numpy as jnp
from jax import lax
from jax.experimental import pallas as pl
from jax.experimental.pallas import tpu as pltpu
from jax.sharding import PartitionSpec as P


F32, BF16 = jnp.float32, jnp.bfloat16
BLK = 256
CORE, Y1, X1, X2, X3 = (1, 0), (2, 0), (4, 0), (8, 0), (12, 0)
Y2, Z1, Z2, Z3 = (0, 1), (0, 2), (0, 4), (0, 6)
LOCAL = ((0, 0), (1, 1), (2, 2), (4, 3), (8, 4))


def send(value, move):
    ways = lax.axis_size("mp")
    mask = move[0] * ways + move[1]
    total = lax.axis_size("dp") * ways
    return lax.ppermute(value, ("dp", "mp"), [(s, s ^ mask) for s in range(total)])


def dot(a, b):
    return jnp.dot(a, b, preferred_element_type=F32)


def dot_nt(a, b):
    return lax.dot_general(a, b, (((1,), (1,)), ((), ())), preferred_element_type=F32)


def dot_tn(a, b):
    return lax.dot_general(a, b, (((0,), (0,)), ((), ())), preferred_element_type=F32)


def place(b):
    return (b // 4) * 2 + b % 2


def cost(flops, moved):
    return pl.CostEstimate(flops=flops, bytes_accessed=moved, transcendentals=0)


def params(dims):
    return pltpu.CompilerParams(dimension_semantics=("arbitrary",) * dims)


def struct(*shape, dtype=BF16):
    return jax.ShapeDtypeStruct(shape, dtype)


def take_half(info, tokens, half):
    rows = tokens.shape[0]

    def body(s_ref, t_ref, o_ref):
        o_ref[...] = t_ref[...]

    return pl.pallas_call(
        body,
        grid_spec=pltpu.PrefetchScalarGridSpec(
            num_scalar_prefetch=1,
            grid=(4,),
            in_specs=[
                pl.BlockSpec((rows, 512), lambda x, s: (0, 2 * x + (((s[0] // 2) % 2) ^ half)))
            ],
            out_specs=pl.BlockSpec((rows, 512), lambda x, s: (0, x)),
        ),
        out_shape=struct(rows, 2048),
        compiler_params=params(1),
        cost_estimate=cost(0, 4 * rows * 2048),
    )(info, tokens)


def down_part(info, tokens, own, mate):
    rows = tokens.shape[0]

    def body(s_ref, ta_ref, tb_ref, fa_ref, fb_ref, o_ref, acc_ref):
        step = pl.program_id(0)
        total = dot(ta_ref[...], fa_ref[0]) + dot(tb_ref[...], fb_ref[0])

        @pl.when(step == 0)
        def _():
            acc_ref[...] = total

        @pl.when(step > 0)
        def _():
            acc_ref[...] += total

        @pl.when(step == 7)
        def _():
            o_ref[...] = acc_ref[...].astype(BF16)

    factor = pl.BlockSpec((1, BLK, BLK), lambda k, s: (k, 0, 0))
    return pl.pallas_call(
        body,
        grid_spec=pltpu.PrefetchScalarGridSpec(
            num_scalar_prefetch=1,
            grid=(8,),
            in_specs=[
                pl.BlockSpec((rows, BLK), lambda k, s: (0, (2 * k) ^ s[0])),
                pl.BlockSpec((rows, BLK), lambda k, s: (0, (2 * k + 1) ^ s[0])),
                factor,
                factor,
            ],
            out_specs=pl.BlockSpec((rows, BLK), lambda k, s: (0, 0)),
            scratch_shapes=[pltpu.VMEM((rows, BLK), F32)],
        ),
        out_shape=struct(rows, BLK),
        compiler_params=params(1),
        cost_estimate=cost(2 * rows * 4096 * BLK, 2 * (rows * 4096 + 4096 * BLK)),
    )(info, tokens, tokens, own, mate)


def forward_half(info, half, tokens, far, weights, down_sum, up_own, up_mate, cotangent, carried):
    rows = tokens.shape[0]

    def body(s_ref, t_ref, r5_ref, r6_ref, r7_ref, w_ref, ds_ref, ua_ref, um_ref, ct_ref, *rest):
        out_ref, g_ref, o5_ref, o6_ref, o7_ref, x_ref, up_ref = rest[-7:]
        xr, cc = pl.program_id(0), pl.program_id(1)
        b = (4 * xr + 2 * half + cc) ^ s_ref[0]
        up = jnp.where(cc == 0, ua_ref[0], um_ref[0])
        hidden = dot_nt(ds_ref[...], up)
        for k, level in LOCAL:
            column = pl.multiple_of((b ^ k) * BLK, BLK)
            hidden += dot(t_ref[:, pl.ds(column, BLK)], w_ref[0, level])
        for level, r_ref in ((5, r5_ref), (6, r6_ref), (7, r7_ref)):
            hidden += dot(r_ref[...], w_ref[0, level])
        live = lax.broadcasted_iota(jnp.int32, (rows, BLK), 0) < s_ref[1]
        scale = 0.7978845608028654
        square = hidden * hidden
        bent = jnp.tanh(scale * hidden * (1.0 + 0.044715 * square))
        half_up = 0.5 * (1.0 + bent)
        slope = half_up + 0.5 * hidden * (1.0 - bent * bent) * scale * (1.0 + 0.134145 * square)
        out_ref[...] = jnp.where(live, hidden * half_up, 0.0).astype(BF16)
        grad = jnp.where(live, ct_ref[...].astype(F32) * slope, 0.0).astype(BF16)
        g_ref[...] = grad
        o5_ref[...] = dot_nt(grad, w_ref[0, 5]).astype(BF16)
        o6_ref[...] = dot_nt(grad, w_ref[0, 6]).astype(BF16)
        o7_ref[...] = dot_nt(grad, w_ref[0, 7]).astype(BF16)
        part = dot(grad, up)
        first = jnp.logical_and(xr == 0, cc == 0)

        @pl.when(first)
        def _():
            up_ref[...] = part

        @pl.when(jnp.logical_not(first))
        def _():
            up_ref[...] += part

        @pl.when(cc == 1)
        def _():
            x_ref[0, 0] = r5_ref[...]
            x_ref[0, 1] = r6_ref[...]
            x_ref[0, 2] = r7_ref[...]
            x_ref[0, 3] = grad

    def b_of(xr, cc, s):
        return (4 * xr + 2 * half + cc) ^ s[0]

    column = pl.BlockSpec((rows, BLK), lambda xr, cc, s: (0, b_of(xr, cc, s)))
    near = pl.BlockSpec((rows, BLK), lambda xr, cc, s: (0, place(b_of(xr, cc, s))))
    factor = pl.BlockSpec((1, BLK, BLK), lambda xr, cc, s: (2 * xr + half, 0, 0))
    fixed = pl.BlockSpec((rows, BLK), lambda xr, cc, s: (0, 0))
    in_specs = [
        pl.BlockSpec((rows, 4096), lambda xr, cc, s: (0, 0)),
        near,
        near,
        near,
        pl.BlockSpec((1, 8, BLK, BLK), lambda xr, cc, s: (b_of(xr, cc, s), 0, 0, 0)),
        fixed,
        factor,
        factor,
        column,
    ]
    operands = [info, tokens, *far, weights, down_sum, up_own, up_mate, cotangent]
    aliases = {}
    if carried is not None:
        in_specs.append(pl.BlockSpec(memory_space=pl.ANY))
        aliases = {len(operands): 0}
        operands.append(carried)
    return pl.pallas_call(
        body,
        grid_spec=pltpu.PrefetchScalarGridSpec(
            num_scalar_prefetch=1,
            grid=(4, 2),
            in_specs=in_specs,
            out_specs=[
                column,
                near,
                near,
                near,
                near,
                pl.BlockSpec((1, 4, rows, BLK), lambda xr, cc, s: (xr, 0, 0, 0)),
                fixed,
            ],
        ),
        out_shape=[
            struct(rows, 4096),
            struct(rows, 2048),
            struct(rows, 2048),
            struct(rows, 2048),
            struct(rows, 2048),
            struct(4, 4, rows, BLK),
            struct(rows, BLK, dtype=F32),
        ],
        input_output_aliases=aliases,
        compiler_params=params(2),
        cost_estimate=cost(8 * 13 * 2 * rows * BLK * BLK, 22 << 20),
    )(*operands)


def grads_of(info, half, xr, tokens, mate_tokens, far, grad, packed, sums, ups, adds, splits):
    rows = tokens.shape[0]
    count = 9 + (2 if ups is not None else 0)

    def body(s_ref, *refs):
        ta, tb = refs[0:5], refs[5:10]
        r5, r6, r7, x_ref, g_ref, da, db = refs[10:17]
        at = 17
        if ups is not None:
            ua, ub = refs[17:19]
            at = 19
        add_refs = refs[at : at + len(adds)]
        out_refs = refs[at + len(adds) :]

        def emit(m, value):
            for (start, size, _), ref in zip(adds, add_refs):
                if start <= m < start + size:
                    value += ref[m - start].astype(F32)
            base = 0
            for size, ref in zip(splits, out_refs):
                if base <= m < base + size:
                    ref[m - base] = value.astype(BF16)
                base += size

        ga, gb = g_ref[...], x_ref[0, 3]
        for level in range(5):
            emit(level, dot_tn(ta[level][...], ga) + dot_tn(tb[level][...], gb))
        for i, r in enumerate((r5, r6, r7)):
            emit(5 + i, dot_tn(r[...], ga) + dot_tn(x_ref[0, i], gb))
        emit(8, dot_tn(ga, da[...]) + dot_tn(gb, db[...]))
        if ups is not None:
            emit(9, dot_tn(ta[0][...], ua[...]) + dot_tn(tb[0][...], ub[...]))
            emit(10, dot_tn(ta[2][...], ua[...]) + dot_tn(tb[2][...], ub[...]))

    def b_of(s):
        return (4 * xr + 2 * half) ^ s[0]

    columns = [
        pl.BlockSpec((rows, BLK), functools.partial(lambda k, i, s: (0, b_of(s) ^ k), k))
        for k, _ in LOCAL
    ]
    near = pl.BlockSpec((rows, BLK), lambda i, s: (0, place(b_of(s))))
    fixed = pl.BlockSpec((rows, BLK), lambda i, s: (0, 0))
    in_specs = columns + columns + [near] * 3
    in_specs += [pl.BlockSpec((1, 4, rows, BLK), lambda i, s: (xr, 0, 0, 0)), near, fixed, fixed]
    operands = [info] + [tokens] * 5 + [mate_tokens] * 5 + list(far) + [packed, grad, *sums]
    if ups is not None:
        in_specs += [fixed, fixed]
        operands += list(ups)
    for _, size, value in adds:
        in_specs.append(pl.BlockSpec((size, BLK, BLK), lambda i, s: (0, 0, 0)))
        operands.append(value)
    return pl.pallas_call(
        body,
        grid_spec=pltpu.PrefetchScalarGridSpec(
            num_scalar_prefetch=1,
            grid=(1,),
            in_specs=in_specs,
            out_specs=[pl.BlockSpec((size, BLK, BLK), lambda i, s: (0, 0, 0)) for size in splits],
        ),
        out_shape=[struct(size, BLK, BLK) for size in splits],
        compiler_params=params(1),
        cost_estimate=cost(count * 4 * rows * BLK * BLK, 4 << 20),
    )(*operands)


def back_half(info, half, same, other, weights, up_sum, down_own, down_mate, from_y, from_z, carried):
    rows = same.shape[0]

    def body(s_ref, same_ref, other_ref, *refs):
        w = refs[0:5]
        us_ref, da_ref, dm_ref, y_ref, z_ref = refs[5:10]
        out_ref = refs[-1]
        xr, cc = pl.program_id(0), pl.program_id(1)
        b = (4 * xr + 2 * half + cc) ^ s_ref[0]
        down = jnp.where(cc == 0, da_ref[0], dm_ref[0])
        total = y_ref[...].astype(F32) + z_ref[...].astype(F32) + dot_nt(us_ref[...], down)
        for (k, level), w_ref in zip(LOCAL, w):
            source = other_ref if k == 2 else same_ref
            column = pl.multiple_of(place(b ^ k) * BLK, BLK)
            total += dot_nt(source[:, pl.ds(column, BLK)], w_ref[0, 0])
        out_ref[...] = total.astype(BF16)

    def b_of(xr, cc, s):
        return (4 * xr + 2 * half + cc) ^ s[0]

    whole = pl.BlockSpec((rows, 2048), lambda xr, cc, s: (0, 0))
    near = pl.BlockSpec((rows, BLK), lambda xr, cc, s: (0, place(b_of(xr, cc, s))))
    factor = pl.BlockSpec((1, BLK, BLK), lambda xr, cc, s: (2 * xr + half, 0, 0))
    in_specs = [whole, whole]
    for k, level in LOCAL:
        in_specs.append(
            pl.BlockSpec(
                (1, 1, BLK, BLK),
                functools.partial(
                    lambda k, level, xr, cc, s: (b_of(xr, cc, s) ^ k, level, 0, 0), k, level
                ),
            )
        )
    in_specs += [pl.BlockSpec((rows, BLK), lambda xr, cc, s: (0, 0)), factor, factor, near, near]
    operands = [info, same, other] + [weights] * 5
    operands += [up_sum, down_own, down_mate, from_y, from_z]
    aliases = {}
    if carried is not None:
        in_specs.append(pl.BlockSpec(memory_space=pl.ANY))
        aliases = {len(operands): 0}
        operands.append(carried)
    return pl.pallas_call(
        body,
        grid_spec=pltpu.PrefetchScalarGridSpec(
            num_scalar_prefetch=1,
            grid=(4, 2),
            in_specs=in_specs,
            out_specs=pl.BlockSpec((rows, BLK), lambda xr, cc, s: (0, b_of(xr, cc, s))),
        ),
        out_shape=struct(rows, 4096),
        input_output_aliases=aliases,
        compiler_params=params(2),
        cost_estimate=cost(8 * 6 * 2 * rows * BLK * BLK, 12 << 20),
    )(*operands)


def gather_factor(shard):
    pair = jnp.stack([shard, send(shard, Y1)])
    own = jnp.concatenate([pair, send(pair, X1), send(pair, X2), send(pair, X3)], 0)
    return own, send(own, CORE)


def sum_over_mp(part):
    def both(a, b):
        return a.astype(F32) + b.astype(F32)

    pair = both(part, send(part, Y2)).astype(BF16)
    total = both(pair, send(pair, Z1)) + both(send(pair, Z2), send(pair, Z3))
    return total.astype(BF16)


def per_device(tokens, block_weights, lowrank_down, lowrank_up, cotangent, seq_lengths):
    me = lax.axis_index("dp").astype(jnp.int32)
    info = jnp.stack([me, seq_lengths[0]])

    def exchange(half):
        with jax.named_scope(f"S_take{half}"):
            mine = take_half(info, tokens, half)
        with jax.named_scope(f"S_far{half}"):
            r5 = send(mine, Y2)
            r6 = send(mine, Z1)
            r7 = send(r6, Z3)
        return r5, r6, r7

    far_a = exchange(1)
    with jax.named_scope("S_agd"):
        down_own, down_mate = gather_factor(lowrank_down)
    with jax.named_scope("S_down"):
        down_sum = sum_over_mp(down_part(info, tokens, down_own, down_mate))
    with jax.named_scope("S_agu"):
        up_own, up_mate = gather_factor(lowrank_up)
    with jax.named_scope("S_mate"):
        mate_tokens = send(tokens, CORE)
        mate_down = send(down_sum, CORE)
    far_b = exchange(0)
    with jax.named_scope("S_fwdA"):
        output, grad_a, a5, a6, a7, pack_a, up_a = forward_half(
            info, 1, tokens, far_a, block_weights, down_sum, up_own, up_mate, cotangent, None
        )
    with jax.named_scope("S_packA"):
        pack_a = send(pack_a, CORE)
    sums = (down_sum, mate_down)

    def grads_a(xr, adds, splits):
        with jax.named_scope(f"S_gradA{xr}"):
            return grads_of(
                info, 1, xr, tokens, mate_tokens, far_a, grad_a, pack_a, sums, None, adds, splits
            )

    with jax.named_scope("S_rsA"):
        low, high = grads_a(2, (), (5, 4))
        low, high = send(low, X1), send(high, X3)
        (right,) = grads_a(1, ((5, 4, high),), (9,))
        (left,) = grads_a(3, ((0, 5, low),), (9,))
        right, left = send(right, X1), send(left, X3)
        (mine_a,) = grads_a(0, ((0, 9, right), (0, 9, left)), (9,))
        across = send(mine_a, Y1)

    def terms_back(t5, t6, t7, name):
        with jax.named_scope(f"S_back{name}"):
            carried = send(t7, Z3)
            from_y = send(t5, Y2)
            from_z = send((t6.astype(F32) + carried.astype(F32)).astype(BF16), Z1)
        return from_y, from_z

    y_a, z_a = terms_back(a5, a6, a7, "A")

    with jax.named_scope("S_fwdB"):
        output, grad_b, b5, b6, b7, pack_b, up_b = forward_half(
            info, 0, tokens, far_b, block_weights, down_sum, up_own, up_mate, cotangent, output
        )
    with jax.named_scope("S_packB"):
        pack_b = send(pack_b, CORE)
    with jax.named_scope("S_up"):
        up_sum = sum_over_mp((up_a + up_b).astype(BF16))
        mate_up = send(up_sum, CORE)
    y_b, z_b = terms_back(b5, b6, b7, "B")

    def grads_b(xr, adds, splits):
        with jax.named_scope(f"S_gradB{xr}"):
            return grads_of(
                info, 0, xr, tokens, mate_tokens, far_b, grad_b, pack_b, sums,
                (up_sum, mate_up), adds, splits,
            )

    with jax.named_scope("S_rsB"):
        low, high = grads_b(2, (), (6, 5))
        low, high = send(low, X1), send(high, X3)
        (right,) = grads_b(1, ((6, 5, high),), (11,))
        (left,) = grads_b(3, ((0, 6, low),), (11,))
        right, left = send(right, X1), send(left, X3)
        (mine_b,) = grads_b(0, ((0, 9, across),), (11,))

    with jax.named_scope("S_backA"):
        grad_tokens = back_half(
            info, 1, grad_a, grad_b, block_weights, up_sum, down_own, down_mate, y_a, z_a, None
        )
    with jax.named_scope("S_backB"):
        grad_tokens = back_half(
            info, 0, grad_b, grad_a, block_weights, up_sum, down_own, down_mate, y_b, z_b, grad_tokens
        )
    with jax.named_scope("S_end"):
        total = mine_b.astype(F32) + right.astype(F32) + left.astype(F32)
        grad_blocks = total[:8].astype(BF16)[None]
        last = send(total[10].astype(BF16), Y1)
        grad_down = (total[9] + last.astype(F32)).astype(BF16)
        grad_lowrank = jnp.stack([grad_down, total[8].astype(BF16)], 1)
    return (output, grad_tokens, grad_blocks, grad_lowrank)


def solution(mesh):
    placed = (
        P("dp", "mp"),
        P("mp", None, None, None),
        P(("mp", "dp"), None),
        P(("mp", "dp"), None),
        P("dp", "mp"),
        P("dp"),
    )
    return jax.shard_map(
        per_device,
        mesh=mesh,
        in_specs=placed,
        out_specs=(
            P("dp", "mp"),
            P("dp", "mp"),
            P(("mp", "dp"), None, None, None),
            P(("mp", "dp"), None, None),
        ),
        check_vma=False,
    )
```

```python
import jax
import jax.numpy as jnp
from jax import lax
from jax.experimental import pallas as pl
from jax.experimental.pallas import tpu as pltpu
from jax.sharding import PartitionSpec as P


F32, BF16 = jnp.float32, jnp.bfloat16
BLK = 256
CORE, Y1, X1, X2, X3 = (1, 0), (2, 0), (4, 0), (8, 0), (12, 0)
Y2, Z1, Z2, Z3 = (0, 1), (0, 2), (0, 4), (0, 6)
LOCAL = ((0, 0), (1, 1), (2, 2), (4, 3), (8, 4))


def send(value, move):
    ways = lax.axis_size("mp")
    mask = move[0] * ways + move[1]
    total = lax.axis_size("dp") * ways
    return lax.ppermute(value, ("dp", "mp"), [(s, s ^ mask) for s in range(total)])


def dot(a, b):
    return jnp.dot(a, b, preferred_element_type=F32)


def dot_nt(a, b):
    return lax.dot_general(a, b, (((1,), (1,)), ((), ())), preferred_element_type=F32)


def dot_tn(a, b):
    return lax.dot_general(a, b, (((0,), (0,)), ((), ())), preferred_element_type=F32)


def place(b):
    return (b // 4) * 2 + b % 2


def cost(flops, moved):
    return pl.CostEstimate(flops=flops, bytes_accessed=moved, transcendentals=0)


def struct(*shape, dtype=BF16):
    return jax.ShapeDtypeStruct(shape, dtype)


def local_call(body, info, operands, out_shape, scratch, flops, moved, aliases=None):
    anywhere = pl.BlockSpec(memory_space=pl.ANY)
    return pl.pallas_call(
        body,
        in_specs=[pl.BlockSpec(memory_space=pltpu.SMEM)] + [anywhere] * len(operands),
        out_specs=[anywhere] * len(out_shape),
        out_shape=out_shape,
        scratch_shapes=scratch,
        input_output_aliases=aliases or {},
        cost_estimate=cost(flops, moved),
    )(info, *operands)


def columns(index, width=BLK):
    return pl.ds(pl.multiple_of(index * width, width), width)


def take_half(info, tokens, half, pieces):
    rows = tokens.shape[0]
    height = rows // pieces
    parts = pieces if pieces > 1 else 0

    def body(s_ref, t_ref, *rest):
        o_ref, part_refs, (buf, sems) = rest[0], rest[1 : 1 + parts], rest[1 + parts :]
        low = ((s_ref[0] // 2) % 2) ^ half
        reads = [
            pltpu.make_async_copy(t_ref.at[:, columns(2 * x + low, 512)], buf.at[x], sems.at[0, x])
            for x in range(4)
        ]
        start_all(reads)
        sent = []
        for x in range(4):
            reads[x].wait()
            to = pl.ds(512 * x, 512)
            writes = [pltpu.make_async_copy(buf.at[x], o_ref.at[:, to], sems.at[1, x])]
            for p, ref in enumerate(part_refs):
                writes.append(
                    pltpu.make_async_copy(
                        buf.at[x, pl.ds(p * height, height)], ref.at[:, to], sems.at[2 + p, x]
                    )
                )
            start_all(writes)
            sent += writes
        wait_all(sent)

    scratch = [pltpu.VMEM((4, rows, 512), BF16), pltpu.SemaphoreType.DMA((2 + parts, 4))]
    out_shape = [struct(rows, 2048)] + [struct(height, 2048)] * parts
    return local_call(body, info, [tokens], out_shape, scratch, 0, 4 * rows * 2048)


def down_part(info, tokens, own, mate):
    rows = tokens.shape[0]

    def body(s_ref, t_ref, fa_ref, fb_ref, o_ref, t, fa, fb, o, sems):
        d = s_ref[0]
        reads = [
            pltpu.make_async_copy(t_ref, t, sems.at[0]),
            pltpu.make_async_copy(fa_ref, fa, sems.at[1]),
            pltpu.make_async_copy(fb_ref, fb, sems.at[2]),
        ]
        for read in reads:
            read.start()
        for read in reads:
            read.wait()
        total = jnp.zeros((rows, BLK), F32)
        for k in range(8):
            total += dot(t[:, columns((2 * k) ^ d)], fa[k])
            total += dot(t[:, columns((2 * k + 1) ^ d)], fb[k])
        o[...] = total.astype(BF16)
        write = pltpu.make_async_copy(o, o_ref, sems.at[3])
        write.start()
        write.wait()

    factor = pltpu.VMEM((8, BLK, BLK), BF16)
    scratch = [
        pltpu.VMEM((rows, 4096), BF16),
        factor,
        factor,
        pltpu.VMEM((rows, BLK), BF16),
        pltpu.SemaphoreType.DMA((4,)),
    ]
    return local_call(
        body, info, [tokens, own, mate], [struct(rows, BLK)], scratch,
        2 * rows * 4096 * BLK, 2 * (rows * 4096 + 4096 * BLK),
    )[0]


def start_all(copies):
    for copy in copies:
        copy.start()


def wait_all(copies):
    for copy in copies:
        copy.wait()


def forward_half(info, half, tokens, far, weights, down_sum, up_own, up_mate, cotangent, carried):
    rows = tokens.shape[0]
    pieces = len(far[1])
    height = rows // pieces

    def body(s_ref, t_ref, r5_ref, *rest):
        r6_refs, r7_refs = rest[:pieces], rest[pieces : 2 * pieces]
        w_ref, ds_ref, ua_ref, um_ref, ct_ref = rest[2 * pieces : 2 * pieces + 5]
        (out_ref, g_ref, o5_ref, o6_ref, o7_ref, x_ref, up_ref,
         t, r, w, ds, u, ct, outs, gs, gone, part, sem_t, sem_r, sem_in, sem_out, sem_one) = rest[-22:]
        d, alive = s_ref[0], s_ref[1]
        rels = [4 * (j // 2) + 2 * half + j % 2 for j in range(8)]
        spots = [columns(place(rel ^ d)) for rel in rels]

        token_reads = [
            pltpu.make_async_copy(t_ref.at[:, columns(rel ^ d)], t.at[rel], sem_t.at[rel])
            for rel in range(16)
        ]
        first = pltpu.make_async_copy(ds_ref, ds, sem_one.at[0])

        def reads(j):
            b = rels[j] ^ d
            factor = um_ref if j % 2 else ua_ref
            copies = [
                pltpu.make_async_copy(w_ref.at[b], w.at[j], sem_in.at[j, 0]),
                pltpu.make_async_copy(ct_ref.at[:, columns(b)], ct.at[j], sem_in.at[j, 1]),
                pltpu.make_async_copy(factor.at[2 * (j // 2) + half], u.at[j], sem_in.at[j, 2]),
                pltpu.make_async_copy(r5_ref.at[:, spots[j]], r.at[j, 0], sem_r.at[j, 0]),
            ]
            for p in range(pieces):
                for i, refs in ((1, r6_refs), (2, r7_refs)):
                    copies.append(
                        pltpu.make_async_copy(
                            refs[p].at[:, spots[j]],
                            r.at[j, i, pl.ds(p * height, height)],
                            sem_r.at[j, 1 + 2 * p + i - 1],
                        )
                    )
            return copies

        def writes(j):
            b = rels[j] ^ d
            pairs = [(outs.at[j], out_ref.at[:, columns(b)]), (gs.at[j], g_ref.at[:, spots[j]])]
            for i, ref in enumerate((o5_ref, o6_ref, o7_ref)):
                pairs.append((gone.at[j, i], ref.at[:, spots[j]]))
            if j % 2:
                pairs += [(r.at[j, i], x_ref.at[j // 2, i]) for i in range(3)]
                pairs.append((gs.at[j], x_ref.at[j // 2, 3]))
            return [pltpu.make_async_copy(a, c, sem_out.at[j, i]) for i, (a, c) in enumerate(pairs)]

        needs = [[rel ^ k for k, _ in LOCAL] for rel in rels]
        order = []
        for j in range(8):
            order.append([k for k in needs[j] if not any(k in o for o in order)])
        first.start()
        for j in range(8):
            start_all([token_reads[k] for k in order[j]])
            start_all(reads(j))
        first.wait()
        sent = []
        for base in (0, 4):
            span = range(base, base + 4)
            for j in span:
                wait_all([token_reads[k] for k in order[j]])
                wait_all(reads(j))
            live = lax.broadcasted_iota(jnp.int32, (rows, BLK), 0) < alive
            scale = 0.7978845608028654
            grads = []
            for j in span:
                fed = [t[k] for k in needs[j]] + [r[j, i] for i in range(3)]
                hidden = dot(jnp.concatenate(fed, 1), w[j].reshape(8 * BLK, BLK))
                hidden += dot_nt(ds[...], u[j])
                square = hidden * hidden
                bent = jnp.tanh(scale * hidden * (1.0 + 0.044715 * square))
                up = 0.5 * (1.0 + bent)
                slope = up + 0.5 * hidden * (1.0 - bent * bent) * scale * (1.0 + 0.134145 * square)
                outs[j] = jnp.where(live, hidden * up, 0.0).astype(BF16)
                gs[j] = jnp.where(live, ct[j].astype(F32) * slope, 0.0).astype(BF16)
            for j in span:
                back = dot_nt(gs[j], w[j, 5:8].reshape(3 * BLK, BLK)).astype(BF16)
                for i in range(3):
                    gone[j, i] = back[:, i * BLK : (i + 1) * BLK]
            grads = jnp.concatenate([gs[j] for j in span], 1)
            total = dot(grads, u[base : base + 4].reshape(4 * BLK, BLK))
            part[...] = total if base == 0 else part[...] + total
            for j in span:
                sent += writes(j)
                start_all(writes(j))
        last = pltpu.make_async_copy(part, up_ref, sem_one.at[1])
        last.start()
        wait_all(sent)
        last.wait()

    operands = [tokens, far[0], *far[1], *far[2], weights, down_sum, up_own, up_mate, cotangent]
    aliases = {}
    if carried is not None:
        aliases = {len(operands) + 1: 0}
        operands.append(carried)
    blocks = pltpu.VMEM((8, rows, BLK), BF16)
    scratch = [
        pltpu.VMEM((16, rows, BLK), BF16),
        pltpu.VMEM((8, 3, rows, BLK), BF16),
        pltpu.VMEM((8, 8, BLK, BLK), BF16),
        pltpu.VMEM((rows, BLK), BF16),
        blocks,
        blocks,
        blocks,
        blocks,
        pltpu.VMEM((8, 3, rows, BLK), BF16),
        pltpu.VMEM((rows, BLK), F32),
        pltpu.SemaphoreType.DMA((16,)),
        pltpu.SemaphoreType.DMA((8, 5)),
        pltpu.SemaphoreType.DMA((8, 3)),
        pltpu.SemaphoreType.DMA((8, 9)),
        pltpu.SemaphoreType.DMA((2,)),
    ]
    out_shape = [struct(rows, 4096)] + [struct(rows, 2048)] * 4
    out_shape += [struct(4, 4, rows, BLK), struct(rows, BLK, dtype=F32)]
    return local_call(
        body, info, operands, out_shape, scratch, 8 * 13 * 2 * rows * BLK * BLK, 22 << 20, aliases
    )


def grads_of(info, half, groups, tokens, mate_tokens, far, grad, packed, sums):
    rows = tokens.shape[0]
    pieces = len(far[1])
    height = rows // pieces
    jobs, sizes = [], []
    for number, group in enumerate(groups):
        at = 0
        for xr, low, high in group:
            for m in range(low, high):
                jobs.append((number, at, xr, m))
                at += 1
        sizes.append(at)
    used = []
    for _, _, xr, _ in jobs:
        if xr not in used:
            used.append(xr)

    def body(s_ref, t_ref, tm_ref, r5_ref, *rest):
        r6_refs, r7_refs = rest[:pieces], rest[pieces : 2 * pieces]
        g_ref, x_ref, da_ref, db_ref = rest[2 * pieces : 2 * pieces + 4]
        out_refs = rest[2 * pieces + 4 : 2 * pieces + 4 + len(sizes)]
        feed, g, ds, outs, sem_f, sem_g, sem_out = rest[-7:]
        d = s_ref[0]

        def block(xr):
            return (4 * xr + 2 * half) ^ d

        top, bottom = pl.ds(0, rows), pl.ds(rows, rows)
        grad_reads = {}
        for i, xr in enumerate(used):
            grad_reads[xr] = [
                pltpu.make_async_copy(
                    g_ref.at[:, columns(place(block(xr)))], g.at[i, top], sem_g.at[i, 0]
                ),
                pltpu.make_async_copy(x_ref.at[xr, 3], g.at[i, bottom], sem_g.at[i, 1]),
            ]
        sum_reads = [
            pltpu.make_async_copy(da_ref, ds.at[top], sem_g.at[4, 0]),
            pltpu.make_async_copy(db_ref, ds.at[bottom], sem_g.at[4, 1]),
        ]

        def reads(n):
            _, _, xr, m = jobs[n]
            if m == 8:
                return []
            if m < 5:
                p = columns(block(xr) ^ LOCAL[m][0])
                pairs = [(t_ref.at[:, p], feed.at[n, top]), (tm_ref.at[:, p], feed.at[n, bottom])]
            else:
                p = columns(place(block(xr)))
                pairs = [(x_ref.at[xr, m - 5], feed.at[n, bottom])]
                if m == 5:
                    pairs.append((r5_ref.at[:, p], feed.at[n, top]))
                else:
                    refs = r6_refs if m == 6 else r7_refs
                    for i in range(pieces):
                        pairs.append(
                            (refs[i].at[:, p], feed.at[n, pl.ds(i * height, height)])
                        )
            return [pltpu.make_async_copy(a, c, sem_f.at[n, i]) for i, (a, c) in enumerate(pairs)]

        started = []
        for n, (_, _, xr, m) in enumerate(jobs):
            if xr not in started:
                started.append(xr)
                start_all(grad_reads[xr])
            start_all(reads(n))
            if n == 0:
                start_all(sum_reads)
        wait_all(sum_reads)
        for xr in used:
            wait_all(grad_reads[xr])
        sent = []
        cut = len(jobs) // 2
        for span in (range(cut), range(cut, len(jobs))):
            for n in span:
                wait_all(reads(n))
            for n in span:
                _, _, xr, m = jobs[n]
                held = g[used.index(xr)]
                value = dot_tn(held, ds[...]) if m == 8 else dot_tn(feed[n], held)
                outs[n] = value.astype(BF16)
            for n in span:
                number, at, _, _ = jobs[n]
                copy = pltpu.make_async_copy(outs.at[n], out_refs[number].at[at], sem_out.at[n])
                copy.start()
                sent.append(copy)
        wait_all(sent)

    count = len(jobs)
    scratch = [
        pltpu.VMEM((count, 2 * rows, BLK), BF16),
        pltpu.VMEM((len(used), 2 * rows, BLK), BF16),
        pltpu.VMEM((2 * rows, BLK), BF16),
        pltpu.VMEM((count, BLK, BLK), BF16),
        pltpu.SemaphoreType.DMA((count, 3)),
        pltpu.SemaphoreType.DMA((5, 2)),
        pltpu.SemaphoreType.DMA((count,)),
    ]
    return local_call(
        body, info, [tokens, mate_tokens, far[0], *far[1], *far[2], grad, packed, *sums],
        [struct(size, BLK, BLK) for size in sizes], scratch,
        count * 4 * rows * BLK * BLK, count * 3 * 2 * rows * BLK,
    )


def down_grads(info, tokens, mate_tokens, ups):
    rows = tokens.shape[0]

    def body(s_ref, t_ref, tm_ref, ua_ref, ub_ref, *rest):
        out_refs = rest[:4]
        feed, up, outs, sem_f, sem_u, sem_out = rest[4:]
        d = s_ref[0]
        top, bottom = pl.ds(0, rows), pl.ds(rows, rows)
        shared = [
            pltpu.make_async_copy(ua_ref, up.at[top], sem_u.at[0]),
            pltpu.make_async_copy(ub_ref, up.at[bottom], sem_u.at[1]),
        ]

        def reads(n):
            p = columns((2 * n) ^ d)
            return [
                pltpu.make_async_copy(t_ref.at[:, p], feed.at[n, top], sem_f.at[n, 0]),
                pltpu.make_async_copy(tm_ref.at[:, p], feed.at[n, bottom], sem_f.at[n, 1]),
            ]

        start_all(shared)
        for n in range(8):
            start_all(reads(n))
        wait_all(shared)
        sent = []
        for n in range(8):
            wait_all(reads(n))
        for n in range(8):
            outs[n] = dot_tn(feed[n], up[...]).astype(BF16)
        for n in range(8):
            copy = pltpu.make_async_copy(outs.at[n], out_refs[n // 2].at[n % 2], sem_out.at[n])
            copy.start()
            sent.append(copy)
        wait_all(sent)

    scratch = [
        pltpu.VMEM((8, 2 * rows, BLK), BF16),
        pltpu.VMEM((2 * rows, BLK), BF16),
        pltpu.VMEM((8, BLK, BLK), BF16),
        pltpu.SemaphoreType.DMA((8, 2)),
        pltpu.SemaphoreType.DMA((2,)),
        pltpu.SemaphoreType.DMA((8,)),
    ]
    return local_call(
        body, info, [tokens, mate_tokens, *ups], [struct(2, BLK, BLK)] * 4, scratch,
        8 * 4 * rows * BLK * BLK, 5 << 20,
    )


def back_all(info, grads, weights, up_sum, down_own, down_mate, from_y, from_z):
    rows = grads[0].shape[0]

    def body(s_ref, g0_ref, g1_ref, w_ref, us_ref, da_ref, dm_ref, y0, y1, z0, z1, out_ref,
             g, w, us, dn, ys, zs, outs, sem_in, sem_out, sem_one):
        d = s_ref[0]
        first = pltpu.make_async_copy(us_ref, us, sem_one.at[0])

        def reads(rel):
            half, p = (rel // 2) % 2, columns(place(rel ^ d))
            return [
                pltpu.make_async_copy((g0_ref, g1_ref)[half].at[:, p], g.at[rel], sem_in.at[rel, 0]),
                pltpu.make_async_copy(
                    w_ref.at[rel ^ d, pl.ds(0, 5)], w.at[rel], sem_in.at[rel, 1]
                ),
            ]

        def extras(rel):
            half, p = (rel // 2) % 2, columns(place(rel ^ d))
            return [
                pltpu.make_async_copy(
                    (da_ref, dm_ref)[rel % 2].at[rel // 2], dn.at[rel], sem_in.at[rel, 2]
                ),
                pltpu.make_async_copy((y0, y1)[half].at[:, p], ys.at[rel], sem_in.at[rel, 3]),
                pltpu.make_async_copy((z0, z1)[half].at[:, p], zs.at[rel], sem_in.at[rel, 4]),
            ]

        first.start()
        order, seen = [], []
        for rel in range(16):
            order.append([rel ^ k for k, _ in LOCAL if rel ^ k not in seen])
            seen += order[-1]
        for rel in range(16):
            for other in order[rel]:
                start_all(reads(other))
            start_all(extras(rel))
        first.wait()
        sent = []
        for base in (0, 4, 8, 12):
            span = range(base, base + 4)
            for rel in span:
                for other in order[rel]:
                    wait_all(reads(other))
                wait_all(extras(rel))
            for rel in span:
                fed = jnp.concatenate([g[rel ^ k] for k, _ in LOCAL] + [us[...]], 1)
                rhs = jnp.concatenate([w[rel ^ k, level] for k, level in LOCAL] + [dn[rel]], 1)
                total = dot_nt(fed, rhs) + ys[rel].astype(F32) + zs[rel].astype(F32)
                outs[rel] = total.astype(BF16)
            for rel in span:
                copy = pltpu.make_async_copy(
                    outs.at[rel], out_ref.at[:, columns(rel ^ d)], sem_out.at[rel]
                )
                copy.start()
                sent.append(copy)
        wait_all(sent)

    operands = [*grads, weights, up_sum, down_own, down_mate, *from_y, *from_z]
    blocks = pltpu.VMEM((16, rows, BLK), BF16)
    scratch = [
        blocks,
        pltpu.VMEM((16, 5, BLK, BLK), BF16),
        pltpu.VMEM((rows, BLK), BF16),
        blocks,
        blocks,
        blocks,
        blocks,
        pltpu.SemaphoreType.DMA((16, 5)),
        pltpu.SemaphoreType.DMA((16,)),
        pltpu.SemaphoreType.DMA((1,)),
    ]
    return local_call(
        body, info, operands, [struct(rows, 4096)], scratch, 16 * 6 * 2 * rows * BLK * BLK, 22 << 20
    )[0]


def after(values, other):
    return lax.optimization_barrier((tuple(values), other))[0]


def gather_factor(shard, other=None):
    pair = jnp.stack([shard, send(shard, Y1)])
    moved = [send(pair, move) for move in (X1, X2, X3)]
    if other is not None:
        moved = list(after(moved, other))
    own = jnp.concatenate([pair] + moved, 0)
    return own, send(own, CORE)


def sum_over_mp(part):
    def both(a, b):
        return a.astype(F32) + b.astype(F32)

    pair = both(part, send(part, Y2)).astype(BF16)
    moved = [send(pair, move) for move in (Z1, Z2, Z3)]
    return (both(pair, moved[0]) + both(moved[1], moved[2])).astype(BF16)


def program(tokens, block_weights, lowrank_down, lowrank_up, cotangent, seq_lengths):
    me = lax.axis_index("dp").astype(jnp.int32)
    info = jnp.stack([me, seq_lengths[0]])

    def exchange(half, pieces):
        mine = take_half(info, tokens, half, pieces)
        whole, parts = mine[0], mine[1:] or mine[:1]
        r5 = send(whole, Y2)
        r6, r7 = [], []
        for p, part in enumerate(parts):
            if p:
                part = lax.optimization_barrier((part, r6[-1]))[0]
            r6.append(send(part, Z1))
            r7.append(send(r6[-1], Z3))
        return r5, r6, r7

    down_own, down_mate = gather_factor(lowrank_down)
    far_a = exchange(1, 2)
    far_b = exchange(0, 1)
    mate_tokens = send(tokens, CORE)
    part = down_part(info, tokens, down_own, down_mate)
    up_own, up_mate = gather_factor(lowrank_up, part)
    down_sum = sum_over_mp(part)
    mate_down = send(down_sum, CORE)
    sums = (down_sum, mate_down)

    def forward(half, far, carried):
        output, grad, t5, t6, t7, pack, up = forward_half(
            info, half, tokens, far, block_weights, down_sum, up_own, up_mate, cotangent, carried
        )
        pack = send(pack, CORE)
        return output, grad, (t5, t6, t7), pack, up

    def terms_back(terms):
        carried = send(terms[2], Z3)
        from_y = send(terms[0], Y2)
        joined = (terms[1].astype(F32) + carried.astype(F32)).astype(BF16)
        return from_y, send(joined, Z1)

    def over_x(half, far, grad, pack):
        fixed = (tokens, mate_tokens, far, grad, pack, sums)
        to1, to3 = grads_of(info, half, (((2, 0, 5), (1, 0, 5)), ((2, 5, 9), (3, 5, 9))), *fixed)
        late1, late3, own = grads_of(info, half, (((1, 5, 9),), ((3, 0, 5),), ((0, 0, 9),)), *fixed)
        got1 = send(to1, X1)
        got3 = send(to3, X3)
        late1 = (late1.astype(F32) + got3[:4].astype(F32)).astype(BF16)
        late3 = (late3.astype(F32) + got1[:5].astype(F32)).astype(BF16)
        end1 = send(late1, X1)
        end3 = send(late3, X3)
        low = own[:5].astype(F32) + got1[5:].astype(F32) + end3.astype(F32)
        high = own[5:].astype(F32) + got3[4:].astype(F32) + end1.astype(F32)
        return low, high

    output, grad_a, terms_a, pack_a, up_a = forward(1, far_a, None)
    y_a, z_a = terms_back(terms_a)
    low_a, high_a = over_x(1, far_a, grad_a, pack_a)
    across = send(jnp.concatenate([low_a, high_a]).astype(BF16), Y1)

    output, grad_b, terms_b, pack_b, up_b = forward(0, far_b, output)
    y_b, z_b = terms_back(terms_b)

    up_sum = sum_over_mp((up_a + up_b).astype(BF16))
    mate_up = send(up_sum, CORE)
    d0, d1, d2, d3 = down_grads(info, tokens, mate_tokens, (up_sum, mate_up))
    low_b, high_b = over_x(0, far_b, grad_b, pack_b)
    d1, d2, d3 = send(d1, X1), send(d2, X2), send(d3, X3)
    downs = d0.astype(F32) + d1.astype(F32) + d2.astype(F32) + d3.astype(F32)
    grad_down = (downs[0] + send(downs[1].astype(BF16), Y1).astype(F32)).astype(BF16)

    grad_tokens = back_all(
        info, (grad_b, grad_a), block_weights, up_sum, down_own, down_mate, (y_b, y_a), (z_b, z_a)
    )
    grad_low = low_b + across[:5].astype(F32)
    grad_high = high_b + across[5:].astype(F32)
    grad_blocks = jnp.concatenate([grad_low, grad_high[:3]]).astype(BF16)[None]
    grad_lowrank = jnp.stack([grad_down, grad_high[3].astype(BF16)], 1)
    return (output, grad_tokens, grad_blocks, grad_lowrank)


def solution(mesh):
    placed = (
        P("dp", "mp"),
        P("mp", None, None, None),
        P(("mp", "dp"), None),
        P(("mp", "dp"), None),
        P("dp", "mp"),
        P("dp"),
    )
    return jax.shard_map(
        program,
        mesh=mesh,
        in_specs=placed,
        out_specs=(
            P("dp", "mp"),
            P("dp", "mp"),
            P(("mp", "dp"), None, None, None),
            P(("mp", "dp"), None, None),
        ),
        check_vma=False,
    )
```

```python
import jax
import jax.numpy as jnp
from jax import lax
from jax.experimental import pallas as pl
from jax.experimental.pallas import tpu as pltpu
from jax.sharding import PartitionSpec as P


F32, BF16 = jnp.float32, jnp.bfloat16
BLK = 256
CORE, Y1, X1, X2, X3 = (1, 0), (2, 0), (4, 0), (8, 0), (12, 0)
Y2, Z1, Z2, Z3 = (0, 1), (0, 2), (0, 4), (0, 6)
LOCAL = ((0, 0), (1, 1), (2, 2), (4, 3), (8, 4))


def send(value, move):
    ways = lax.axis_size("mp")
    mask = move[0] * ways + move[1]
    total = lax.axis_size("dp") * ways
    return lax.ppermute(value, ("dp", "mp"), [(s, s ^ mask) for s in range(total)])


def dot(a, b):
    return jnp.dot(a, b, preferred_element_type=F32)


def dot_nt(a, b):
    return lax.dot_general(a, b, (((1,), (1,)), ((), ())), preferred_element_type=F32)


def dot_tn(a, b):
    return lax.dot_general(a, b, (((0,), (0,)), ((), ())), preferred_element_type=F32)


def place(b):
    return (b // 4) * 2 + b % 2


def cost(flops, moved):
    return pl.CostEstimate(flops=flops, bytes_accessed=moved, transcendentals=0)


def struct(*shape, dtype=BF16):
    return jax.ShapeDtypeStruct(shape, dtype)


def local_call(body, info, operands, out_shape, scratch, flops, moved, aliases=None):
    anywhere = pl.BlockSpec(memory_space=pl.ANY)
    return pl.pallas_call(
        body,
        in_specs=[pl.BlockSpec(memory_space=pltpu.SMEM)] + [anywhere] * len(operands),
        out_specs=[anywhere] * len(out_shape),
        out_shape=out_shape,
        scratch_shapes=scratch,
        input_output_aliases=aliases or {},
        cost_estimate=cost(flops, moved),
    )(info, *operands)


def columns(index, width=BLK):
    return pl.ds(pl.multiple_of(index * width, width), width)


def take_half(info, tokens, half, pieces):
    rows = tokens.shape[0]
    height = rows // pieces
    parts = pieces if pieces > 1 else 0

    def body(s_ref, t_ref, *rest):
        o_ref, part_refs, (buf, sems) = rest[0], rest[1 : 1 + parts], rest[1 + parts :]
        low = ((s_ref[0] // 2) % 2) ^ half
        reads = [
            pltpu.make_async_copy(t_ref.at[:, columns(2 * x + low, 512)], buf.at[x], sems.at[0, x])
            for x in range(4)
        ]
        start_all(reads)
        sent = []
        for x in range(4):
            reads[x].wait()
            to = pl.ds(512 * x, 512)
            writes = [pltpu.make_async_copy(buf.at[x], o_ref.at[:, to], sems.at[1, x])]
            for p, ref in enumerate(part_refs):
                writes.append(
                    pltpu.make_async_copy(
                        buf.at[x, pl.ds(p * height, height)], ref.at[:, to], sems.at[2 + p, x]
                    )
                )
            start_all(writes)
            sent += writes
        wait_all(sent)

    scratch = [pltpu.VMEM((4, rows, 512), BF16), pltpu.SemaphoreType.DMA((2 + parts, 4))]
    out_shape = [struct(rows, 2048)] + [struct(height, 2048)] * parts
    return local_call(body, info, [tokens], out_shape, scratch, 0, 4 * rows * 2048)


def down_part(info, tokens, own, mate):
    rows = tokens.shape[0]

    def body(s_ref, t_ref, fa_ref, fb_ref, o_ref, t, fa, fb, o, sems):
        d = s_ref[0]
        reads = [
            pltpu.make_async_copy(t_ref, t, sems.at[0]),
            pltpu.make_async_copy(fa_ref, fa, sems.at[1]),
            pltpu.make_async_copy(fb_ref, fb, sems.at[2]),
        ]
        for read in reads:
            read.start()
        for read in reads:
            read.wait()
        total = jnp.zeros((rows, BLK), F32)
        for k in range(8):
            total += dot(t[:, columns((2 * k) ^ d)], fa[k])
            total += dot(t[:, columns((2 * k + 1) ^ d)], fb[k])
        o[...] = total.astype(BF16)
        write = pltpu.make_async_copy(o, o_ref, sems.at[3])
        write.start()
        write.wait()

    factor = pltpu.VMEM((8, BLK, BLK), BF16)
    scratch = [
        pltpu.VMEM((rows, 4096), BF16),
        factor,
        factor,
        pltpu.VMEM((rows, BLK), BF16),
        pltpu.SemaphoreType.DMA((4,)),
    ]
    return local_call(
        body, info, [tokens, own, mate], [struct(rows, BLK)], scratch,
        2 * rows * 4096 * BLK, 2 * (rows * 4096 + 4096 * BLK),
    )[0]


def start_all(copies):
    for copy in copies:
        copy.start()


def wait_all(copies):
    for copy in copies:
        copy.wait()


def forward_half(info, half, tokens, far, weights, down_sum, up_own, up_mate, cotangent, carried):
    rows = tokens.shape[0]
    pieces = len(far[1])
    height = rows // pieces

    def body(s_ref, t_ref, r5_ref, *rest):
        r6_refs, r7_refs = rest[:pieces], rest[pieces : 2 * pieces]
        w_ref, ds_ref, ua_ref, um_ref, ct_ref = rest[2 * pieces : 2 * pieces + 5]
        (out_ref, g_ref, o5_ref, o6_ref, o7_ref, x_ref, up_ref,
         t, r, w, ds, u, ct, outs, gs, gone, part, sem_t, sem_r, sem_in, sem_out, sem_one) = rest[-22:]
        d, alive = s_ref[0], s_ref[1]

        def rel_of(j):
            return 4 * (j // 2) + 2 * half + j % 2

        def spot(j):
            return columns(place(rel_of(j) ^ d))

        token_reads = [
            pltpu.make_async_copy(t_ref.at[:, columns(rel ^ d)], t.at[rel], sem_t.at[rel])
            for rel in range(16)
        ]
        first = pltpu.make_async_copy(ds_ref, ds, sem_one.at[0])

        def reads(j, parity):
            b = rel_of(j) ^ d
            factor = (ua_ref, um_ref)[parity]
            copies = [
                pltpu.make_async_copy(w_ref.at[b], w.at[j], sem_in.at[j, 0]),
                pltpu.make_async_copy(ct_ref.at[:, columns(b)], ct.at[j], sem_in.at[j, 1]),
                pltpu.make_async_copy(factor.at[2 * (j // 2) + half], u.at[j], sem_in.at[j, 2]),
                pltpu.make_async_copy(r5_ref.at[:, spot(j)], r.at[j, 0], sem_r.at[j, 0]),
            ]
            for p in range(pieces):
                for i, refs in ((1, r6_refs), (2, r7_refs)):
                    copies.append(
                        pltpu.make_async_copy(
                            refs[p].at[:, spot(j)],
                            r.at[j, i, pl.ds(p * height, height)],
                            sem_r.at[j, 1 + 2 * p + i - 1],
                        )
                    )
            return copies

        def writes(j, parity):
            b = rel_of(j) ^ d
            pairs = [(outs.at[j], out_ref.at[:, columns(b)]), (gs.at[j], g_ref.at[:, spot(j)])]
            for i, ref in enumerate((o5_ref, o6_ref, o7_ref)):
                pairs.append((gone.at[j, i], ref.at[:, spot(j)]))
            if parity:
                pairs.append((gs.at[j], x_ref.at[j // 2]))
            return [pltpu.make_async_copy(a, c, sem_out.at[j, i]) for i, (a, c) in enumerate(pairs)]

        first.start()
        start_all(token_reads)
        for j in range(8):
            start_all(reads(j, j % 2))
        first.wait()
        wait_all(token_reads)

        def group(base, carry):
            js = [4 * base + i for i in range(4)]
            for i, j in enumerate(js):
                wait_all(reads(j, i % 2))
            live = lax.broadcasted_iota(jnp.int32, (rows, BLK), 0) < alive
            scale = 0.7978845608028654
            for i, j in enumerate(js):
                within = 4 * (i // 2) + 2 * half + i % 2
                fed = [t[8 * (base ^ (k // 8)) + (within ^ (k % 8))] for k, _ in LOCAL]
                fed += [r[j, n] for n in range(3)]
                hidden = dot(jnp.concatenate(fed, 1), w[j].reshape(8 * BLK, BLK))
                hidden += dot_nt(ds[...], u[j])
                square = hidden * hidden
                bent = jnp.tanh(scale * hidden * (1.0 + 0.044715 * square))
                up = 0.5 * (1.0 + bent)
                slope = up + 0.5 * hidden * (1.0 - bent * bent) * scale * (1.0 + 0.134145 * square)
                outs[j] = jnp.where(live, hidden * up, 0.0).astype(BF16)
                gs[j] = jnp.where(live, ct[j].astype(F32) * slope, 0.0).astype(BF16)
            for j in js:
                back = dot_nt(gs[j], w[j, 5:8].reshape(3 * BLK, BLK)).astype(BF16)
                for i in range(3):
                    gone[j, i] = back[:, i * BLK : (i + 1) * BLK]
            grads = jnp.concatenate([gs[j] for j in js], 1)
            factors = jnp.concatenate([u[j] for j in js], 0)
            part[...] = jnp.where(base == 0, 0.0, part[...]) + dot(grads, factors)
            for i, j in enumerate(js):
                start_all(writes(j, i % 2))
            return carry

        part[...] = jnp.zeros_like(part)
        lax.fori_loop(0, 2, group, 0)
        sent = []
        for j in range(8):
            sent += writes(j, j % 2)
        last = pltpu.make_async_copy(part, up_ref, sem_one.at[1])
        last.start()
        wait_all(sent)
        last.wait()

    operands = [tokens, far[0], *far[1], *far[2], weights, down_sum, up_own, up_mate, cotangent]
    aliases = {}
    if carried is not None:
        aliases = {len(operands) + 1: 0}
        operands.append(carried)
    blocks = pltpu.VMEM((8, rows, BLK), BF16)
    scratch = [
        pltpu.VMEM((16, rows, BLK), BF16),
        pltpu.VMEM((8, 3, rows, BLK), BF16),
        pltpu.VMEM((8, 8, BLK, BLK), BF16),
        pltpu.VMEM((rows, BLK), BF16),
        blocks,
        blocks,
        blocks,
        blocks,
        pltpu.VMEM((8, 3, rows, BLK), BF16),
        pltpu.VMEM((rows, BLK), F32),
        pltpu.SemaphoreType.DMA((16,)),
        pltpu.SemaphoreType.DMA((8, 5)),
        pltpu.SemaphoreType.DMA((8, 3)),
        pltpu.SemaphoreType.DMA((8, 9)),
        pltpu.SemaphoreType.DMA((2,)),
    ]
    out_shape = [struct(rows, 4096)] + [struct(rows, 2048)] * 4
    out_shape += [struct(4, rows, BLK), struct(rows, BLK, dtype=F32)]
    return local_call(
        body, info, operands, out_shape, scratch, 8 * 13 * 2 * rows * BLK * BLK, 22 << 20, aliases
    )


def grads_of(info, half, groups, tokens, mate_tokens, far, mate_far, grad, packed, sums):
    rows = tokens.shape[0]
    pieces = len(far[1])
    jobs, sizes = [], []
    for number, group in enumerate(groups):
        at = 0
        for xr, low, high in group:
            for m in range(low, high):
                jobs.append((number, at, xr, m))
                at += 1
        sizes.append(at)
    used = []
    for _, _, xr, _ in jobs:
        if xr not in used:
            used.append(xr)

    def body(s_ref, t_ref, tm_ref, *rest):
        remote = []
        for i in range(2):
            flat = rest[i * (1 + 2 * pieces) : (i + 1) * (1 + 2 * pieces)]
            remote.append((flat[:1], flat[1 : 1 + pieces], flat[1 + pieces :]))
        rest = rest[2 * (1 + 2 * pieces) :]
        g_ref, x_ref, da_ref, db_ref = rest[:4]
        out_refs = rest[4 : 4 + len(sizes)]
        feed, g, ds, outs, sem_f, sem_g, sem_out = rest[-7:]
        d = s_ref[0]

        def block(xr):
            return (4 * xr + 2 * half) ^ d

        top, bottom = pl.ds(0, rows), pl.ds(rows, rows)
        grad_reads = {}
        for i, xr in enumerate(used):
            grad_reads[xr] = [
                pltpu.make_async_copy(
                    g_ref.at[:, columns(place(block(xr)))], g.at[i, top], sem_g.at[i, 0]
                ),
                pltpu.make_async_copy(x_ref.at[xr], g.at[i, bottom], sem_g.at[i, 1]),
            ]
        sum_reads = [
            pltpu.make_async_copy(da_ref, ds.at[top], sem_g.at[4, 0]),
            pltpu.make_async_copy(db_ref, ds.at[bottom], sem_g.at[4, 1]),
        ]

        def reads(n):
            _, _, xr, m = jobs[n]
            if m == 8:
                return []
            if m < 5:
                p = columns(block(xr) ^ LOCAL[m][0])
                pairs = [(t_ref.at[:, p], feed.at[n, top]), (tm_ref.at[:, p], feed.at[n, bottom])]
            else:
                p = columns(place(block(xr)))
                pairs = []
                for i in range(2):
                    refs = remote[i][m - 5]
                    tall = rows // len(refs)
                    for q, ref in enumerate(refs):
                        pairs.append((ref.at[:, p], feed.at[n, pl.ds(i * rows + q * tall, tall)]))
            return [pltpu.make_async_copy(a, c, sem_f.at[n, i]) for i, (a, c) in enumerate(pairs)]

        started = []
        for n, (_, _, xr, m) in enumerate(jobs):
            if xr not in started:
                started.append(xr)
                start_all(grad_reads[xr])
            start_all(reads(n))
            if n == 0:
                start_all(sum_reads)
        wait_all(sum_reads)
        for xr in used:
            wait_all(grad_reads[xr])
        sent = []
        cut = len(jobs) // 2
        for span in (range(cut), range(cut, len(jobs))):
            for n in span:
                wait_all(reads(n))
            for n in span:
                _, _, xr, m = jobs[n]
                held = g[used.index(xr)]
                value = dot_tn(held, ds[...]) if m == 8 else dot_tn(feed[n], held)
                outs[n] = value.astype(BF16)
            for n in span:
                number, at, _, _ = jobs[n]
                copy = pltpu.make_async_copy(outs.at[n], out_refs[number].at[at], sem_out.at[n])
                copy.start()
                sent.append(copy)
        wait_all(sent)

    count = len(jobs)
    scratch = [
        pltpu.VMEM((count, 2 * rows, BLK), BF16),
        pltpu.VMEM((len(used), 2 * rows, BLK), BF16),
        pltpu.VMEM((2 * rows, BLK), BF16),
        pltpu.VMEM((count, BLK, BLK), BF16),
        pltpu.SemaphoreType.DMA((count, 4)),
        pltpu.SemaphoreType.DMA((5, 2)),
        pltpu.SemaphoreType.DMA((count,)),
    ]
    return local_call(
        body, info,
        [tokens, mate_tokens, far[0], *far[1], *far[2], mate_far[0], *mate_far[1], *mate_far[2],
         grad, packed, *sums],
        [struct(size, BLK, BLK) for size in sizes], scratch,
        count * 4 * rows * BLK * BLK, count * 3 * 2 * rows * BLK,
    )


def down_grads(info, tokens, mate_tokens, ups):
    rows = tokens.shape[0]

    def body(s_ref, t_ref, tm_ref, ua_ref, ub_ref, *rest):
        out_refs = rest[:4]
        feed, up, outs, sem_f, sem_u, sem_out = rest[4:]
        d = s_ref[0]
        top, bottom = pl.ds(0, rows), pl.ds(rows, rows)
        shared = [
            pltpu.make_async_copy(ua_ref, up.at[top], sem_u.at[0]),
            pltpu.make_async_copy(ub_ref, up.at[bottom], sem_u.at[1]),
        ]

        def reads(n):
            p = columns((2 * n) ^ d)
            return [
                pltpu.make_async_copy(t_ref.at[:, p], feed.at[n, top], sem_f.at[n, 0]),
                pltpu.make_async_copy(tm_ref.at[:, p], feed.at[n, bottom], sem_f.at[n, 1]),
            ]

        start_all(shared)
        for n in range(8):
            start_all(reads(n))
        wait_all(shared)
        sent = []
        for n in range(8):
            wait_all(reads(n))

        def group(base, carry):
            for i in range(4):
                outs[4 * base + i] = dot_tn(feed[4 * base + i], up[...]).astype(BF16)
            return carry

        lax.fori_loop(0, 2, group, 0)
        for n in range(8):
            copy = pltpu.make_async_copy(outs.at[n], out_refs[n // 2].at[n % 2], sem_out.at[n])
            copy.start()
            sent.append(copy)
        wait_all(sent)

    scratch = [
        pltpu.VMEM((8, 2 * rows, BLK), BF16),
        pltpu.VMEM((2 * rows, BLK), BF16),
        pltpu.VMEM((8, BLK, BLK), BF16),
        pltpu.SemaphoreType.DMA((8, 2)),
        pltpu.SemaphoreType.DMA((2,)),
        pltpu.SemaphoreType.DMA((8,)),
    ]
    return local_call(
        body, info, [tokens, mate_tokens, *ups], [struct(2, BLK, BLK)] * 4, scratch,
        8 * 4 * rows * BLK * BLK, 5 << 20,
    )


def back_all(info, grads, weights, up_sum, down_own, down_mate, from_y, from_z):
    rows = grads[0].shape[0]

    def body(s_ref, g0_ref, g1_ref, w_ref, us_ref, da_ref, dm_ref, y0, y1, z0, z1, out_ref,
             g, w, us, dn, ys, zs, outs, sem_in, sem_out, sem_one):
        d = s_ref[0]
        first = pltpu.make_async_copy(us_ref, us, sem_one.at[0])

        def reads(rel):
            half, p = (rel // 2) % 2, columns(place(rel ^ d))
            return [
                pltpu.make_async_copy((g0_ref, g1_ref)[half].at[:, p], g.at[rel], sem_in.at[rel, 0]),
                pltpu.make_async_copy(
                    w_ref.at[rel ^ d, pl.ds(0, 5)], w.at[rel], sem_in.at[rel, 1]
                ),
            ]

        def extras(rel):
            half, p = (rel // 2) % 2, columns(place(rel ^ d))
            return [
                pltpu.make_async_copy(
                    (da_ref, dm_ref)[rel % 2].at[rel // 2], dn.at[rel], sem_in.at[rel, 2]
                ),
                pltpu.make_async_copy((y0, y1)[half].at[:, p], ys.at[rel], sem_in.at[rel, 3]),
                pltpu.make_async_copy((z0, z1)[half].at[:, p], zs.at[rel], sem_in.at[rel, 4]),
            ]

        first.start()
        for rel in range(16):
            start_all(reads(rel))
            start_all(extras(rel))
        first.wait()
        for rel in range(16):
            wait_all(reads(rel))
            wait_all(extras(rel))

        def write(rel):
            return pltpu.make_async_copy(
                outs.at[rel], out_ref.at[:, columns(rel ^ d)], sem_out.at[rel]
            )

        def group(xr, carry):
            for low in range(4):
                others = [4 * (xr ^ (k // 4)) + (low ^ (k % 4)) for k, _ in LOCAL]
                rel = 4 * xr + low
                fed = jnp.concatenate([g[o] for o in others] + [us[...]], 1)
                rhs = [w[o, level] for o, (_, level) in zip(others, LOCAL)] + [dn[rel]]
                total = dot_nt(fed, jnp.concatenate(rhs, 1))
                total += ys[rel].astype(F32) + zs[rel].astype(F32)
                outs[rel] = total.astype(BF16)
            for low in range(4):
                write(4 * xr + low).start()
            return carry

        lax.fori_loop(0, 4, group, 0)
        for rel in range(16):
            write(rel).wait()

    operands = [*grads, weights, up_sum, down_own, down_mate, *from_y, *from_z]
    blocks = pltpu.VMEM((16, rows, BLK), BF16)
    scratch = [
        blocks,
        pltpu.VMEM((16, 5, BLK, BLK), BF16),
        pltpu.VMEM((rows, BLK), BF16),
        blocks,
        blocks,
        blocks,
        blocks,
        pltpu.SemaphoreType.DMA((16, 5)),
        pltpu.SemaphoreType.DMA((16,)),
        pltpu.SemaphoreType.DMA((1,)),
    ]
    return local_call(
        body, info, operands, [struct(rows, 4096)], scratch, 16 * 6 * 2 * rows * BLK * BLK, 22 << 20
    )[0]


def after(values, other):
    return lax.optimization_barrier((tuple(values), other))[0]


def gather_factor(shard, other=None):
    pair = jnp.stack([shard, send(shard, Y1)])
    moved = [send(pair, move) for move in (X1, X2, X3)]
    if other is not None:
        moved = list(after(moved, other))
    own = jnp.concatenate([pair] + moved, 0)
    return own, send(own, CORE)


def sum_over_mp(part, after_pair=None):
    def both(a, b):
        return a.astype(F32) + b.astype(F32)

    pair = both(part, send(part, Y2)).astype(BF16)
    if after_pair is not None:
        after_pair.append(pair)
    moved = [send(pair, move) for move in (Z1, Z2, Z3)]
    return (both(pair, moved[0]) + both(moved[1], moved[2])).astype(BF16)


def program(tokens, block_weights, lowrank_down, lowrank_up, cotangent, seq_lengths):
    me = lax.axis_index("dp").astype(jnp.int32)
    info = jnp.stack([me, seq_lengths[0]])

    def exchange(half, pieces):
        mine = take_half(info, tokens, half, pieces)
        whole, parts = mine[0], mine[1:] or mine[:1]
        r5 = send(whole, Y2)
        r6, r7 = [], []
        for p, part in enumerate(parts):
            if p:
                part = lax.optimization_barrier((part, r6[-1]))[0]
            r6.append(send(part, Z1))
            r7.append(send(r6[-1], Z3))
        return r5, r6, r7

    far_a = exchange(1, 2)
    down_own, down_mate = gather_factor(lowrank_down, far_a[1][0])
    far_b = exchange(0, 1)
    mate_tokens = send(tokens, CORE)
    part = down_part(info, tokens, down_own, down_mate)
    marks = []
    down_sum = sum_over_mp(part, marks)
    up_own, up_mate = gather_factor(lowrank_up, marks[0])
    mate_down = send(down_sum, CORE)
    sums = (down_sum, mate_down)

    def to_mate(far):
        return (
            send(far[0], CORE), [send(v, CORE) for v in far[1]], [send(v, CORE) for v in far[2]]
        )

    mate_a, mate_b = to_mate(far_a), to_mate(far_b)

    def forward(half, far, carried):
        output, grad, t5, t6, t7, pack, up = forward_half(
            info, half, tokens, far, block_weights, down_sum, up_own, up_mate, cotangent, carried
        )
        pack = send(pack, CORE)
        return output, grad, (t5, t6, t7), pack, up

    def terms_back(terms, other):
        carried = send(terms[2], Z3)
        from_y = send(terms[0], Y2)
        carried = after((carried,), other)[0]
        joined = (terms[1].astype(F32) + carried.astype(F32)).astype(BF16)
        return from_y, send(joined, Z1)

    def local_grads(half, far, mate_far, grad, pack):
        fixed = (tokens, mate_tokens, far, mate_far, grad, pack, sums)
        gone = grads_of(info, half, (((2, 0, 5), (1, 0, 5)), ((2, 5, 9), (3, 5, 9))), *fixed)
        rest = grads_of(info, half, (((1, 5, 9),), ((3, 0, 5),), ((0, 0, 9),)), *fixed)
        return gone, rest

    def over_x(gone, rest, extra, other):
        to1, to3 = gone
        late1, late3, own = rest
        got1 = send(to1, X1)
        got3 = send(to3, X3)
        got1, got3 = after((got1, got3), other)
        late1 = (late1.astype(F32) + got3[:4].astype(F32)).astype(BF16)
        late3 = (late3.astype(F32) + got1[:5].astype(F32)).astype(BF16)
        if extra:
            late1 = jnp.concatenate([late1, extra[0]])
            late3 = jnp.concatenate([late3, extra[1]])
        end1 = send(late1, X1)
        end3 = send(late3, X3)
        low = own[:5].astype(F32) + got1[5:].astype(F32) + end3[:5].astype(F32)
        high = own[5:].astype(F32) + got3[4:].astype(F32) + end1[:4].astype(F32)
        return low, high, end1[4:], end3[5:]

    output, grad_a, terms_a, pack_a, up_a = forward(1, far_a, None)
    gone_a, rest_a = local_grads(1, far_a, mate_a, grad_a, pack_a)
    y_a, z_a = terms_back(terms_a, rest_a[0])

    output, grad_b, terms_b, pack_b, up_b = forward(0, far_b, output)
    low_a, high_a, _, _ = over_x(gone_a, rest_a, None, up_b)
    gone_b, rest_b = local_grads(0, far_b, mate_b, grad_b, pack_b)
    y_b, z_b = terms_back(terms_b, rest_b[0])
    low_a, high_a = after((low_a, high_a), rest_b[0])
    across = send(jnp.concatenate([low_a, high_a]).astype(BF16), Y1)

    up_sum = sum_over_mp((up_a + up_b).astype(BF16))
    mate_up = send(up_sum, CORE)
    d0, d1, d2, d3 = down_grads(info, tokens, mate_tokens, (up_sum, mate_up))
    d2 = send(d2, X2)
    low_b, high_b, d1, d3 = over_x(gone_b, rest_b, (d1, d3), d0)
    downs = d0.astype(F32) + d1.astype(F32) + d2.astype(F32) + d3.astype(F32)
    grad_down = (downs[0] + send(downs[1].astype(BF16), Y1).astype(F32)).astype(BF16)

    grad_tokens = back_all(
        info, (grad_b, grad_a), block_weights, up_sum, down_own, down_mate, (y_b, y_a), (z_b, z_a)
    )
    grad_low = low_b + across[:5].astype(F32)
    grad_high = high_b + across[5:].astype(F32)
    grad_blocks = jnp.concatenate([grad_low, grad_high[:3]]).astype(BF16)[None]
    grad_lowrank = jnp.stack([grad_down, grad_high[3].astype(BF16)], 1)
    return (output, grad_tokens, grad_blocks, grad_lowrank)


def solution(mesh):
    placed = (
        P("dp", "mp"),
        P("mp", None, None, None),
        P(("mp", "dp"), None),
        P(("mp", "dp"), None),
        P("dp", "mp"),
        P("dp"),
    )
    return jax.shard_map(
        program,
        mesh=mesh,
        in_specs=placed,
        out_specs=(
            P("dp", "mp"),
            P("dp", "mp"),
            P(("mp", "dp"), None, None, None),
            P(("mp", "dp"), None, None),
        ),
        check_vma=False,
    )
```

```python
import jax
import jax.numpy as jnp
from jax import lax
from jax.experimental import pallas as pl
from jax.experimental.pallas import tpu as pltpu
from jax.sharding import PartitionSpec as P


F32, BF16 = jnp.float32, jnp.bfloat16
BLK = 256
CORE, Y1, X1, X2, X3 = (1, 0), (2, 0), (4, 0), (8, 0), (12, 0)
Y2, Z1, Z2, Z3 = (0, 1), (0, 2), (0, 4), (0, 6)
LOCAL = ((0, 0), (1, 1), (2, 2), (4, 3), (8, 4))


def send(value, move):
    ways = lax.axis_size("mp")
    mask = move[0] * ways + move[1]
    total = lax.axis_size("dp") * ways
    return lax.ppermute(value, ("dp", "mp"), [(s, s ^ mask) for s in range(total)])


def dot(a, b):
    return jnp.dot(a, b, preferred_element_type=F32)


def dot_nt(a, b):
    return lax.dot_general(a, b, (((1,), (1,)), ((), ())), preferred_element_type=F32)


def dot_tn(a, b):
    return lax.dot_general(a, b, (((0,), (0,)), ((), ())), preferred_element_type=F32)


def place(b):
    return (b // 4) * 2 + b % 2


def cost(flops, moved):
    return pl.CostEstimate(flops=flops, bytes_accessed=moved, transcendentals=0)


def struct(*shape, dtype=BF16):
    return jax.ShapeDtypeStruct(shape, dtype)


def local_call(body, info, operands, out_shape, scratch, flops, moved, aliases=None):
    anywhere = pl.BlockSpec(memory_space=pl.ANY)
    return pl.pallas_call(
        body,
        in_specs=[pl.BlockSpec(memory_space=pltpu.SMEM)] + [anywhere] * len(operands),
        out_specs=[anywhere] * len(out_shape),
        out_shape=out_shape,
        scratch_shapes=scratch,
        input_output_aliases=aliases or {},
        cost_estimate=cost(flops, moved),
    )(info, *operands)


def columns(index, width=BLK):
    return pl.ds(pl.multiple_of(index * width, width), width)


def take_half(info, tokens, half, pieces):
    rows = tokens.shape[0]
    height = rows // pieces
    parts = pieces if pieces > 1 else 0

    def body(s_ref, t_ref, *rest):
        o_ref, part_refs, (buf, sems) = rest[0], rest[1 : 1 + parts], rest[1 + parts :]
        low = ((s_ref[0] // 2) % 2) ^ half
        reads = [
            pltpu.make_async_copy(t_ref.at[:, columns(2 * x + low, 512)], buf.at[x], sems.at[0, x])
            for x in range(4)
        ]
        start_all(reads)
        sent = []
        for x in range(4):
            reads[x].wait()
            to = pl.ds(512 * x, 512)
            writes = [pltpu.make_async_copy(buf.at[x], o_ref.at[:, to], sems.at[1, x])]
            for p, ref in enumerate(part_refs):
                writes.append(
                    pltpu.make_async_copy(
                        buf.at[x, pl.ds(p * height, height)], ref.at[:, to], sems.at[2 + p, x]
                    )
                )
            start_all(writes)
            sent += writes
        wait_all(sent)

    scratch = [pltpu.VMEM((4, rows, 512), BF16), pltpu.SemaphoreType.DMA((2 + parts, 4))]
    out_shape = [struct(rows, 2048)] + [struct(height, 2048)] * parts
    return local_call(body, info, [tokens], out_shape, scratch, 0, 4 * rows * 2048)


def down_part(info, tokens, own, mate):
    rows = tokens.shape[0]

    def body(s_ref, t_ref, *rest):
        f_refs, (o_ref, t, f, o, sems) = rest[:8], rest[8:]
        d = s_ref[0]
        reads = [pltpu.make_async_copy(t_ref, t, sems.at[8])]
        for i, ref in enumerate(f_refs):
            reads.append(pltpu.make_async_copy(ref, f.at[i], sems.at[i]))
        for read in reads:
            read.start()
        for read in reads:
            read.wait()
        total = jnp.zeros((rows, BLK), F32)
        for i in range(8):
            for low in range(2):
                rel = 4 * (i % 4) + 2 * low + i // 4
                total += dot(t[:, columns(rel ^ d)], f[i, low])
        o[...] = total.astype(BF16)
        write = pltpu.make_async_copy(o, o_ref, sems.at[9])
        write.start()
        write.wait()

    scratch = [
        pltpu.VMEM((rows, 4096), BF16),
        pltpu.VMEM((8, 2, BLK, BLK), BF16),
        pltpu.VMEM((rows, BLK), BF16),
        pltpu.SemaphoreType.DMA((10,)),
    ]
    return local_call(
        body, info, [tokens, *own, *mate], [struct(rows, BLK)], scratch,
        2 * rows * 4096 * BLK, 2 * (rows * 4096 + 4096 * BLK),
    )[0]


def start_all(copies):
    for copy in copies:
        copy.start()


def wait_all(copies):
    for copy in copies:
        copy.wait()


def forward_half(info, half, tokens, far, weights, down_sum, up_own, up_mate, cotangent, carried):
    rows = tokens.shape[0]
    pieces = len(far[1])
    height = rows // pieces

    def body(s_ref, t_ref, r5_ref, *rest):
        r6_refs, r7_refs = rest[:pieces], rest[pieces : 2 * pieces]
        w_ref, ds_ref = rest[2 * pieces : 2 * pieces + 2]
        u_refs = rest[2 * pieces + 2 : 2 * pieces + 10]
        ct_ref = rest[2 * pieces + 10]
        (out_ref, g_ref, o5_ref, o6_ref, o7_ref, x_ref, up_ref,
         t, r, w, ds, u, ct, outs, gs, gone, part, sem_t, sem_r, sem_in, sem_out, sem_one) = rest[-22:]
        d, alive = s_ref[0], s_ref[1]

        def rel_of(j):
            return 4 * (j // 2) + 2 * half + j % 2

        def spot(j):
            return columns(place(rel_of(j) ^ d))

        token_reads = [
            pltpu.make_async_copy(t_ref.at[:, columns(rel ^ d)], t.at[rel], sem_t.at[rel])
            for rel in range(16)
        ]
        first = pltpu.make_async_copy(ds_ref, ds, sem_one.at[0])

        def reads(j, parity):
            b = rel_of(j) ^ d
            factor = u_refs[4 * parity + j // 2 if isinstance(j, int) else 0]
            copies = [
                pltpu.make_async_copy(w_ref.at[b], w.at[j], sem_in.at[j, 0]),
                pltpu.make_async_copy(ct_ref.at[:, columns(b)], ct.at[j], sem_in.at[j, 1]),
                pltpu.make_async_copy(factor.at[half], u.at[j], sem_in.at[j, 2]),
                pltpu.make_async_copy(r5_ref.at[:, spot(j)], r.at[j, 0], sem_r.at[j, 0]),
            ]
            for p in range(pieces):
                for i, refs in ((1, r6_refs), (2, r7_refs)):
                    copies.append(
                        pltpu.make_async_copy(
                            refs[p].at[:, spot(j)],
                            r.at[j, i, pl.ds(p * height, height)],
                            sem_r.at[j, 1 + 2 * p + i - 1],
                        )
                    )
            return copies

        def writes(j, parity):
            b = rel_of(j) ^ d
            pairs = [(outs.at[j], out_ref.at[:, columns(b)]), (gs.at[j], g_ref.at[:, spot(j)])]
            for i, ref in enumerate((o5_ref, o6_ref, o7_ref)):
                pairs.append((gone.at[j, i], ref.at[:, spot(j)]))
            if parity:
                pairs.append((gs.at[j], x_ref.at[j // 2]))
            return [pltpu.make_async_copy(a, c, sem_out.at[j, i]) for i, (a, c) in enumerate(pairs)]

        first.start()
        start_all(token_reads)
        for j in range(8):
            start_all(reads(j, j % 2))
        first.wait()
        wait_all(token_reads)

        def group(base, carry):
            js = [4 * base + i for i in range(4)]
            for i, j in enumerate(js):
                wait_all(reads(j, i % 2))
            live = lax.broadcasted_iota(jnp.int32, (rows, BLK), 0) < alive
            scale = 0.7978845608028654
            for i, j in enumerate(js):
                within = 4 * (i // 2) + 2 * half + i % 2
                fed = [t[8 * (base ^ (k // 8)) + (within ^ (k % 8))] for k, _ in LOCAL]
                fed += [r[j, n] for n in range(3)]
                hidden = dot(jnp.concatenate(fed, 1), w[j].reshape(8 * BLK, BLK))
                hidden += dot_nt(ds[...], u[j])
                square = hidden * hidden
                bent = jnp.tanh(scale * hidden * (1.0 + 0.044715 * square))
                up = 0.5 * (1.0 + bent)
                slope = up + 0.5 * hidden * (1.0 - bent * bent) * scale * (1.0 + 0.134145 * square)
                outs[j] = jnp.where(live, hidden * up, 0.0).astype(BF16)
                gs[j] = jnp.where(live, ct[j].astype(F32) * slope, 0.0).astype(BF16)
            for j in js:
                back = dot_nt(gs[j], w[j, 5:8].reshape(3 * BLK, BLK)).astype(BF16)
                for i in range(3):
                    gone[j, i] = back[:, i * BLK : (i + 1) * BLK]
            grads = jnp.concatenate([gs[j] for j in js], 1)
            factors = jnp.concatenate([u[j] for j in js], 0)
            part[...] = jnp.where(base == 0, 0.0, part[...]) + dot(grads, factors)
            for i, j in enumerate(js):
                start_all(writes(j, i % 2))
            return carry

        part[...] = jnp.zeros_like(part)
        lax.fori_loop(0, 2, group, 0)
        sent = []
        for j in range(8):
            sent += writes(j, j % 2)
        last = pltpu.make_async_copy(part, up_ref, sem_one.at[1])
        last.start()
        wait_all(sent)
        last.wait()

    operands = [tokens, far[0], *far[1], *far[2], weights, down_sum, *up_own, *up_mate, cotangent]
    aliases = {}
    if carried is not None:
        aliases = {len(operands) + 1: 0}
        operands.append(carried)
    blocks = pltpu.VMEM((8, rows, BLK), BF16)
    scratch = [
        pltpu.VMEM((16, rows, BLK), BF16),
        pltpu.VMEM((8, 3, rows, BLK), BF16),
        pltpu.VMEM((8, 8, BLK, BLK), BF16),
        pltpu.VMEM((rows, BLK), BF16),
        blocks,
        blocks,
        blocks,
        blocks,
        pltpu.VMEM((8, 3, rows, BLK), BF16),
        pltpu.VMEM((rows, BLK), F32),
        pltpu.SemaphoreType.DMA((16,)),
        pltpu.SemaphoreType.DMA((8, 5)),
        pltpu.SemaphoreType.DMA((8, 3)),
        pltpu.SemaphoreType.DMA((8, 9)),
        pltpu.SemaphoreType.DMA((2,)),
    ]
    out_shape = [struct(rows, 4096)] + [struct(rows, 2048)] * 4
    out_shape += [struct(4, rows, BLK), struct(rows, BLK, dtype=F32)]
    return local_call(
        body, info, operands, out_shape, scratch, 8 * 13 * 2 * rows * BLK * BLK, 22 << 20, aliases
    )


def grads_of(info, half, groups, tokens, mate_tokens, far, mate_far, grad, packed, sums):
    rows = tokens.shape[0]
    pieces = len(far[1])
    jobs, sizes = [], []
    for number, group in enumerate(groups):
        at = 0
        for xr, low, high in group:
            for m in range(low, high):
                jobs.append((number, at, xr, m))
                at += 1
        sizes.append(at)
    used = []
    for _, _, xr, _ in jobs:
        if xr not in used:
            used.append(xr)

    def body(s_ref, t_ref, tm_ref, *rest):
        remote = []
        for i in range(2):
            flat = rest[i * (1 + 2 * pieces) : (i + 1) * (1 + 2 * pieces)]
            remote.append((flat[:1], flat[1 : 1 + pieces], flat[1 + pieces :]))
        rest = rest[2 * (1 + 2 * pieces) :]
        g_ref, x_ref, da_ref, db_ref = rest[:4]
        out_refs = rest[4 : 4 + len(sizes)]
        feed, held, outs, sem_f, sem_h, sem_out = rest[-6:]
        d = s_ref[0]

        def block(xr):
            return (4 * xr + 2 * half) ^ d

        top, bottom = pl.ds(0, rows), pl.ds(rows, rows)

        def grad_pairs(xr, to):
            return [
                (g_ref.at[:, columns(place(block(xr)))], to.at[top]),
                (x_ref.at[xr], to.at[bottom]),
            ]

        shared = []
        for i, xr in enumerate(used):
            for n, (source, to) in enumerate(grad_pairs(xr, held.at[i])):
                shared.append(pltpu.make_async_copy(source, to, sem_h.at[i, n]))
        for n, (source, where) in enumerate(((da_ref, top), (db_ref, bottom))):
            shared.append(
                pltpu.make_async_copy(source, held.at[len(used), where], sem_h.at[len(used), n])
            )

        def reads(n):
            _, _, xr, m = jobs[n]
            if m == 8:
                pairs = grad_pairs(xr, feed.at[n])
            elif m < 5:
                p = columns(block(xr) ^ LOCAL[m][0])
                pairs = [(t_ref.at[:, p], feed.at[n, top]), (tm_ref.at[:, p], feed.at[n, bottom])]
            else:
                p = columns(place(block(xr)))
                pairs = []
                for i in range(2):
                    refs = remote[i][m - 5]
                    tall = rows // len(refs)
                    for q, ref in enumerate(refs):
                        pairs.append((ref.at[:, p], feed.at[n, pl.ds(i * rows + q * tall, tall)]))
            return [pltpu.make_async_copy(a, c, sem_f.at[n]) for a, c in pairs]

        start_all(shared)
        for n in range(len(jobs)):
            start_all(reads(n))
        wait_all(shared)
        slots = [len(used) if m == 8 else used.index(xr) for _, _, xr, m in jobs]
        cut = len(jobs) // 2

        def part(i, carry):
            for q in range(cut):
                whole = feed.at[cut * i + q]
                pltpu.make_async_copy(whole, whole, sem_f.at[cut * i + q]).wait()
            for q in range(cut):
                slot = jnp.where(i == 0, slots[q], slots[cut + q])
                outs[cut * i + q] = dot_tn(feed[cut * i + q], held[slot]).astype(BF16)
            return carry

        lax.fori_loop(0, 2, part, 0)
        sent = []
        for n, (number, at, _, _) in enumerate(jobs):
            sent.append(pltpu.make_async_copy(outs.at[n], out_refs[number].at[at], sem_out.at[n]))
        start_all(sent)
        wait_all(sent)

    count = len(jobs)
    scratch = [
        pltpu.VMEM((count, 2 * rows, BLK), BF16),
        pltpu.VMEM((len(used) + 1, 2 * rows, BLK), BF16),
        pltpu.VMEM((count, BLK, BLK), BF16),
        pltpu.SemaphoreType.DMA((count,)),
        pltpu.SemaphoreType.DMA((len(used) + 1, 2)),
        pltpu.SemaphoreType.DMA((count,)),
    ]
    return local_call(
        body, info,
        [tokens, mate_tokens, far[0], *far[1], *far[2], mate_far[0], *mate_far[1], *mate_far[2],
         grad, packed, *sums],
        [struct(size, BLK, BLK) for size in sizes], scratch,
        count * 4 * rows * BLK * BLK, count * 3 * 2 * rows * BLK,
    )


def down_grads(info, tokens, mate_tokens, ups):
    rows = tokens.shape[0]

    def body(s_ref, t_ref, tm_ref, ua_ref, ub_ref, *rest):
        out_refs = rest[:4]
        feed, up, outs, sem_f, sem_u, sem_out = rest[4:]
        d = s_ref[0]
        top, bottom = pl.ds(0, rows), pl.ds(rows, rows)
        shared = [
            pltpu.make_async_copy(ua_ref, up.at[top], sem_u.at[0]),
            pltpu.make_async_copy(ub_ref, up.at[bottom], sem_u.at[1]),
        ]

        def reads(n):
            p = columns((2 * n) ^ d)
            return [
                pltpu.make_async_copy(t_ref.at[:, p], feed.at[n, top], sem_f.at[n, 0]),
                pltpu.make_async_copy(tm_ref.at[:, p], feed.at[n, bottom], sem_f.at[n, 1]),
            ]

        start_all(shared)
        for n in range(8):
            start_all(reads(n))
        wait_all(shared)
        sent = []
        for n in range(8):
            wait_all(reads(n))

        def group(base, carry):
            for i in range(4):
                outs[4 * base + i] = dot_tn(feed[4 * base + i], up[...]).astype(BF16)
            return carry

        lax.fori_loop(0, 2, group, 0)
        for n in range(8):
            copy = pltpu.make_async_copy(outs.at[n], out_refs[n // 2].at[n % 2], sem_out.at[n])
            copy.start()
            sent.append(copy)
        wait_all(sent)

    scratch = [
        pltpu.VMEM((8, 2 * rows, BLK), BF16),
        pltpu.VMEM((2 * rows, BLK), BF16),
        pltpu.VMEM((8, BLK, BLK), BF16),
        pltpu.SemaphoreType.DMA((8, 2)),
        pltpu.SemaphoreType.DMA((2,)),
        pltpu.SemaphoreType.DMA((8,)),
    ]
    return local_call(
        body, info, [tokens, mate_tokens, *ups], [struct(2, BLK, BLK)] * 4, scratch,
        8 * 4 * rows * BLK * BLK, 5 << 20,
    )


def back_all(info, grads, weights, up_sum, down_own, down_mate, from_y, from_z):
    rows = grads[0].shape[0]

    def body(s_ref, g0_ref, g1_ref, w_ref, us_ref, *rest):
        d_refs, (y0, y1, z0, z1, out_ref) = rest[:8], rest[8:13]
        g, w, us, dn, ys, zs, outs, sem_in, sem_out, sem_one = rest[13:]
        d = s_ref[0]
        first = pltpu.make_async_copy(us_ref, us, sem_one.at[0])

        def reads(rel):
            half, p = (rel // 2) % 2, columns(place(rel ^ d))
            return [
                pltpu.make_async_copy((g0_ref, g1_ref)[half].at[:, p], g.at[rel], sem_in.at[rel, 0]),
                pltpu.make_async_copy(
                    w_ref.at[rel ^ d, pl.ds(0, 5)], w.at[rel], sem_in.at[rel, 1]
                ),
            ]

        def extras(rel):
            half, p = (rel // 2) % 2, columns(place(rel ^ d))
            return [
                pltpu.make_async_copy(
                    d_refs[4 * (rel % 2) + rel // 4].at[(rel // 2) % 2], dn.at[rel], sem_in.at[rel, 2]
                ),
                pltpu.make_async_copy((y0, y1)[half].at[:, p], ys.at[rel], sem_in.at[rel, 3]),
                pltpu.make_async_copy((z0, z1)[half].at[:, p], zs.at[rel], sem_in.at[rel, 4]),
            ]

        first.start()
        for rel in range(16):
            start_all(reads(rel))
            start_all(extras(rel))
        first.wait()
        for rel in range(16):
            wait_all(reads(rel))
            wait_all(extras(rel))

        def write(rel):
            return pltpu.make_async_copy(
                outs.at[rel], out_ref.at[:, columns(rel ^ d)], sem_out.at[rel]
            )

        def group(xr, carry):
            for low in range(4):
                others = [4 * (xr ^ (k // 4)) + (low ^ (k % 4)) for k, _ in LOCAL]
                rel = 4 * xr + low
                fed = jnp.concatenate([g[o] for o in others] + [us[...]], 1)
                rhs = [w[o, level] for o, (_, level) in zip(others, LOCAL)] + [dn[rel]]
                total = dot_nt(fed, jnp.concatenate(rhs, 1))
                total += ys[rel].astype(F32) + zs[rel].astype(F32)
                outs[rel] = total.astype(BF16)
            for low in range(4):
                write(4 * xr + low).start()
            return carry

        lax.fori_loop(0, 4, group, 0)
        for rel in range(16):
            write(rel).wait()

    operands = [*grads, weights, up_sum, *down_own, *down_mate, *from_y, *from_z]
    blocks = pltpu.VMEM((16, rows, BLK), BF16)
    scratch = [
        blocks,
        pltpu.VMEM((16, 5, BLK, BLK), BF16),
        pltpu.VMEM((rows, BLK), BF16),
        blocks,
        blocks,
        blocks,
        blocks,
        pltpu.SemaphoreType.DMA((16, 5)),
        pltpu.SemaphoreType.DMA((16,)),
        pltpu.SemaphoreType.DMA((1,)),
    ]
    return local_call(
        body, info, operands, [struct(rows, 4096)], scratch, 16 * 6 * 2 * rows * BLK * BLK, 22 << 20
    )[0]


def after(values, other):
    return lax.optimization_barrier((tuple(values), other))[0]


def gather_factor(shard, other=None):
    pair = jnp.stack([shard, send(shard, Y1)])
    moved = [send(pair, move) for move in (X1, X2, X3)]
    if other is not None:
        moved = list(after(moved, other))
    own = [pair] + moved
    return own, [send(piece, CORE) for piece in own]


def sum_over_mp(part, after_pair=None):
    def both(a, b):
        return a.astype(F32) + b.astype(F32)

    pair = both(part, send(part, Y2)).astype(BF16)
    if after_pair is not None:
        after_pair.append(pair)
    moved = [send(pair, move) for move in (Z1, Z2, Z3)]
    return (both(pair, moved[0]) + both(moved[1], moved[2])).astype(BF16)


def program(tokens, block_weights, lowrank_down, lowrank_up, cotangent, seq_lengths):
    me = lax.axis_index("dp").astype(jnp.int32)
    info = jnp.stack([me, seq_lengths[0]])

    def exchange(half, pieces):
        mine = take_half(info, tokens, half, pieces)
        whole, parts = mine[0], mine[1:] or mine[:1]
        r5 = send(whole, Y2)
        r6, r7 = [], []
        for part in parts:
            r6.append(send(part, Z1))
            r7.append(send(r6[-1], Z3))
        return r5, r6, r7

    far_a = exchange(1, 2)
    down_own, down_mate = gather_factor(lowrank_down)
    far_b = exchange(0, 1)
    mate_tokens = send(tokens, CORE)
    part = down_part(info, tokens, down_own, down_mate)
    marks = []
    down_sum = sum_over_mp(part, marks)
    up_own, up_mate = gather_factor(lowrank_up, marks[0])
    mate_down = send(down_sum, CORE)
    sums = (down_sum, mate_down)

    def to_mate(far):
        return (
            send(far[0], CORE), [send(v, CORE) for v in far[1]], [send(v, CORE) for v in far[2]]
        )

    mate_a, mate_b = to_mate(far_a), to_mate(far_b)

    def forward(half, far, carried):
        output, grad, t5, t6, t7, pack, up = forward_half(
            info, half, tokens, far, block_weights, down_sum, up_own, up_mate, cotangent, carried
        )
        pack = send(pack, CORE)
        return output, grad, (t5, t6, t7), pack, up

    def terms_back(terms, other):
        carried = send(terms[2], Z3)
        from_y = send(terms[0], Y2)
        carried = after((carried,), other)[0]
        joined = (terms[1].astype(F32) + carried.astype(F32)).astype(BF16)
        return from_y, send(joined, Z1)

    def local_grads(half, far, mate_far, grad, pack):
        fixed = (tokens, mate_tokens, far, mate_far, grad, pack, sums)
        gone = grads_of(info, half, (((2, 0, 5), (1, 0, 5)), ((2, 5, 9), (3, 5, 9))), *fixed)
        rest = grads_of(info, half, (((1, 5, 9),), ((3, 0, 5),), ((0, 0, 5),), ((0, 5, 9),)), *fixed)
        return gone, rest

    def over_x(gone, rest, extra, other):
        to1, to3 = gone
        late1, late3, own_low, own_high = rest
        got1 = send(to1, X1)
        got3 = send(to3, X3)
        got1, got3 = after((got1, got3), other)
        late1 = (late1.astype(F32) + got3[:4].astype(F32)).astype(BF16)
        late3 = (late3.astype(F32) + got1[:5].astype(F32)).astype(BF16)
        if extra:
            late1 = jnp.concatenate([late1, extra[0]])
            late3 = jnp.concatenate([late3, extra[1]])
        end1 = send(late1, X1)
        end3 = send(late3, X3)
        low = own_low.astype(F32) + got1[5:].astype(F32) + end3[:5].astype(F32)
        high = own_high.astype(F32) + got3[4:].astype(F32) + end1[:4].astype(F32)
        return low, high, end1[4:], end3[5:]

    output, grad_a, terms_a, pack_a, up_a = forward(1, far_a, None)
    gone_a, rest_a = local_grads(1, far_a, mate_a, grad_a, pack_a)
    y_a, z_a = terms_back(terms_a, rest_a[0])

    output, grad_b, terms_b, pack_b, up_b = forward(0, far_b, output)
    low_a, high_a, _, _ = over_x(gone_a, rest_a, None, up_b)
    gone_b, rest_b = local_grads(0, far_b, mate_b, grad_b, pack_b)
    y_b, z_b = terms_back(terms_b, rest_b[0])
    low_a, high_a = after((low_a, high_a), rest_b[0])
    across = send(jnp.concatenate([low_a, high_a]).astype(BF16), Y1)

    up_sum = sum_over_mp((up_a + up_b).astype(BF16))
    mate_up = send(up_sum, CORE)
    d0, d1, d2, d3 = down_grads(info, tokens, mate_tokens, (up_sum, mate_up))
    d2 = send(d2, X2)
    low_b, high_b, d1, d3 = over_x(gone_b, rest_b, (d1, d3), d0)
    downs = d0.astype(F32) + d1.astype(F32) + d2.astype(F32) + d3.astype(F32)
    grad_down = (downs[0] + send(downs[1].astype(BF16), Y1).astype(F32)).astype(BF16)

    grad_tokens = back_all(
        info, (grad_b, grad_a), block_weights, up_sum, down_own, down_mate, (y_b, y_a), (z_b, z_a)
    )
    grad_low = low_b + across[:5].astype(F32)
    grad_high = high_b + across[5:].astype(F32)
    grad_blocks = jnp.concatenate([grad_low, grad_high[:3]]).astype(BF16)[None]
    grad_lowrank = jnp.stack([grad_down, grad_high[3].astype(BF16)], 1)
    return (output, grad_tokens, grad_blocks, grad_lowrank)


def solution(mesh):
    placed = (
        P("dp", "mp"),
        P("mp", None, None, None),
        P(("mp", "dp"), None),
        P(("mp", "dp"), None),
        P("dp", "mp"),
        P("dp"),
    )
    return jax.shard_map(
        program,
        mesh=mesh,
        in_specs=placed,
        out_specs=(
            P("dp", "mp"),
            P("dp", "mp"),
            P(("mp", "dp"), None, None, None),
            P(("mp", "dp"), None, None),
        ),
        check_vma=False,
    )
```

```python
import jax
import jax.numpy as jnp
from jax import lax
from jax.experimental import pallas as pl
from jax.experimental.pallas import tpu as pltpu
from jax.sharding import PartitionSpec as P


F32, BF16 = jnp.float32, jnp.bfloat16
BLK = 256
CORE, Y1, X1, X2, X3 = (1, 0), (2, 0), (4, 0), (8, 0), (12, 0)
Y2, Z1, Z2, Z3 = (0, 1), (0, 2), (0, 4), (0, 6)
LOCAL = ((0, 0), (1, 1), (2, 2), (4, 3), (8, 4))


def send(value, move):
    ways = lax.axis_size("mp")
    mask = move[0] * ways + move[1]
    total = lax.axis_size("dp") * ways
    return lax.ppermute(value, ("dp", "mp"), [(s, s ^ mask) for s in range(total)])


def dot(a, b):
    return jnp.dot(a, b, preferred_element_type=F32)


def dot_nt(a, b):
    return lax.dot_general(a, b, (((1,), (1,)), ((), ())), preferred_element_type=F32)


def dot_tn(a, b):
    return lax.dot_general(a, b, (((0,), (0,)), ((), ())), preferred_element_type=F32)


def place(b):
    return (b // 4) * 2 + b % 2


def cost(flops, moved):
    return pl.CostEstimate(flops=flops, bytes_accessed=moved, transcendentals=0)


def struct(*shape, dtype=BF16):
    return jax.ShapeDtypeStruct(shape, dtype)


def local_call(body, info, operands, out_shape, scratch, flops, moved, aliases=None):
    anywhere = pl.BlockSpec(memory_space=pl.ANY)
    return pl.pallas_call(
        body,
        in_specs=[pl.BlockSpec(memory_space=pltpu.SMEM)] + [anywhere] * len(operands),
        out_specs=[anywhere] * len(out_shape),
        out_shape=out_shape,
        scratch_shapes=scratch,
        input_output_aliases=aliases or {},
        cost_estimate=cost(flops, moved),
    )(info, *operands)


def columns(index, width=BLK):
    return pl.ds(pl.multiple_of(index * width, width), width)


def take_halves(info, tokens):
    rows = tokens.shape[0]
    height = rows // 2

    def body(s_ref, t_ref, a_ref, p0_ref, p1_ref, b_ref, buf, sems):
        own = (s_ref[0] // 2) % 2

        def read(half, x):
            piece = columns(2 * x + (own ^ half), 512)
            return pltpu.make_async_copy(t_ref.at[:, piece], buf.at[half, x], sems.at[0, half, x])

        def writes(half, x):
            to = pl.ds(512 * x, 512)
            if not half:
                return [pltpu.make_async_copy(buf.at[0, x], b_ref.at[:, to], sems.at[1, 0, x])]
            pairs = [(buf.at[1, x], a_ref)]
            pairs.append((buf.at[1, x, pl.ds(0, height)], p0_ref))
            pairs.append((buf.at[1, x, pl.ds(height, height)], p1_ref))
            return [
                pltpu.make_async_copy(a, ref.at[:, to], sems.at[1 + i, 1, x])
                for i, (a, ref) in enumerate(pairs)
            ]

        steps = [(half, x) for half in (1, 0) for x in range(4)]
        for step in steps:
            read(*step).start()
        sent = []
        for step in steps:
            read(*step).wait()
            sent += writes(*step)
            start_all(writes(*step))
        wait_all(sent)

    scratch = [pltpu.VMEM((2, 4, rows, 512), BF16), pltpu.SemaphoreType.DMA((4, 2, 4))]
    out_shape = [struct(rows, 2048), struct(height, 2048), struct(height, 2048), struct(rows, 2048)]
    return local_call(body, info, [tokens], out_shape, scratch, 0, 10 * rows * 2048)


def down_part(info, tokens, own, mate):
    rows = tokens.shape[0]

    def body(s_ref, t_ref, *rest):
        f_refs, (o_ref, t, f, o, sems) = rest[:8], rest[8:]
        d = s_ref[0]
        reads = [pltpu.make_async_copy(t_ref, t, sems.at[8])]
        for i, ref in enumerate(f_refs):
            reads.append(pltpu.make_async_copy(ref.at[0], f.at[i], sems.at[i]))
        for read in reads:
            read.start()
        for read in reads:
            read.wait()
        total = jnp.zeros((rows, BLK), F32)
        for i in range(8):
            for low in range(2):
                rel = 4 * (i % 4) + 2 * low + i // 4
                total += dot(t[:, columns(rel ^ d)], f[i, low])
        o[...] = total.astype(BF16)
        write = pltpu.make_async_copy(o, o_ref, sems.at[9])
        write.start()
        write.wait()

    scratch = [
        pltpu.VMEM((rows, 4096), BF16),
        pltpu.VMEM((8, 2, BLK, BLK), BF16),
        pltpu.VMEM((rows, BLK), BF16),
        pltpu.SemaphoreType.DMA((10,)),
    ]
    return local_call(
        body, info, [tokens, *own, *mate], [struct(rows, BLK)], scratch,
        2 * rows * 4096 * BLK, 2 * (rows * 4096 + 4096 * BLK),
    )[0]


def start_all(copies):
    for copy in copies:
        copy.start()


def wait_all(copies):
    for copy in copies:
        copy.wait()


def forward_half(info, half, tokens, far, weights, down_sum, up_own, up_mate, cotangent, carried):
    rows = tokens.shape[0]
    pieces = len(far[1])
    height = rows // pieces

    def body(s_ref, t_ref, r5_ref, *rest):
        r6_refs, r7_refs = rest[:pieces], rest[pieces : 2 * pieces]
        w_ref, ds_ref = rest[2 * pieces : 2 * pieces + 2]
        u_refs = rest[2 * pieces + 2 : 2 * pieces + 10]
        ct_ref = rest[2 * pieces + 10]
        (out_ref, g_ref, o5_ref, o6_ref, o7_ref, x_ref, up_ref,
         t, r, w, ds, u, ct, outs, gs, gone, part, sem_t, sem_r, sem_in, sem_out, sem_one) = rest[-22:]
        d, alive = s_ref[0], s_ref[1]

        def rel_of(j):
            return 4 * (j // 2) + 2 * half + j % 2

        def spot(j):
            return columns(place(rel_of(j) ^ d))

        token_reads = [
            pltpu.make_async_copy(t_ref.at[:, columns(rel ^ d)], t.at[rel], sem_t.at[rel])
            for rel in range(16)
        ]
        first = pltpu.make_async_copy(ds_ref, ds, sem_one.at[0])

        def reads(j, parity):
            b = rel_of(j) ^ d
            factor = u_refs[4 * parity + j // 2 if isinstance(j, int) else 0]
            copies = [
                pltpu.make_async_copy(w_ref.at[b], w.at[j], sem_in.at[j, 0]),
                pltpu.make_async_copy(ct_ref.at[:, columns(b)], ct.at[j], sem_in.at[j, 1]),
                pltpu.make_async_copy(factor.at[1, half], u.at[j], sem_in.at[j, 2]),
                pltpu.make_async_copy(r5_ref.at[:, spot(j)], r.at[j, 0], sem_r.at[j, 0]),
            ]
            for p in range(pieces):
                for i, refs in ((1, r6_refs), (2, r7_refs)):
                    copies.append(
                        pltpu.make_async_copy(
                            refs[p].at[:, spot(j)],
                            r.at[j, i, pl.ds(p * height, height)],
                            sem_r.at[j, 1 + 2 * p + i - 1],
                        )
                    )
            return copies

        def writes(j, parity):
            b = rel_of(j) ^ d
            pairs = [(outs.at[j], out_ref.at[:, columns(b)]), (gs.at[j], g_ref.at[:, spot(j)])]
            for i, ref in enumerate((o5_ref, o6_ref, o7_ref)):
                pairs.append((gone.at[j, i], ref.at[:, spot(j)]))
            if parity:
                pairs.append((gs.at[j], x_ref.at[j // 2]))
            return [pltpu.make_async_copy(a, c, sem_out.at[j, i]) for i, (a, c) in enumerate(pairs)]

        first.start()
        start_all(token_reads)
        for j in range(8):
            start_all(reads(j, j % 2))
        first.wait()
        wait_all(token_reads)

        def group(base, carry):
            js = [4 * base + i for i in range(4)]
            for i, j in enumerate(js):
                wait_all(reads(j, i % 2))
            live = lax.broadcasted_iota(jnp.int32, (rows, BLK), 0) < alive
            scale = 0.7978845608028654
            for i, j in enumerate(js):
                within = 4 * (i // 2) + 2 * half + i % 2
                fed = [t[8 * (base ^ (k // 8)) + (within ^ (k % 8))] for k, _ in LOCAL]
                fed += [r[j, n] for n in range(3)]
                hidden = dot(jnp.concatenate(fed, 1), w[j].reshape(8 * BLK, BLK))
                hidden += dot_nt(ds[...], u[j])
                square = hidden * hidden
                bent = jnp.tanh(scale * hidden * (1.0 + 0.044715 * square))
                up = 0.5 * (1.0 + bent)
                slope = up + 0.5 * hidden * (1.0 - bent * bent) * scale * (1.0 + 0.134145 * square)
                outs[j] = jnp.where(live, hidden * up, 0.0).astype(BF16)
                gs[j] = jnp.where(live, ct[j].astype(F32) * slope, 0.0).astype(BF16)
            for j in js:
                back = dot_nt(gs[j], w[j, 5:8].reshape(3 * BLK, BLK)).astype(BF16)
                for i in range(3):
                    gone[j, i] = back[:, i * BLK : (i + 1) * BLK]
            grads = jnp.concatenate([gs[j] for j in js], 1)
            factors = jnp.concatenate([u[j] for j in js], 0)
            part[...] = jnp.where(base == 0, 0.0, part[...]) + dot(grads, factors)
            for i, j in enumerate(js):
                start_all(writes(j, i % 2))
            return carry

        part[...] = jnp.zeros_like(part)
        lax.fori_loop(0, 2, group, 0)
        sent = []
        for j in range(8):
            sent += writes(j, j % 2)
        last = pltpu.make_async_copy(part, up_ref, sem_one.at[1])
        last.start()
        wait_all(sent)
        last.wait()

    operands = [tokens, far[0], *far[1], *far[2], weights, down_sum, *up_own, *up_mate, cotangent]
    aliases = {}
    if carried is not None:
        aliases = {len(operands) + 1: 0}
        operands.append(carried)
    blocks = pltpu.VMEM((8, rows, BLK), BF16)
    scratch = [
        pltpu.VMEM((16, rows, BLK), BF16),
        pltpu.VMEM((8, 3, rows, BLK), BF16),
        pltpu.VMEM((8, 8, BLK, BLK), BF16),
        pltpu.VMEM((rows, BLK), BF16),
        blocks,
        blocks,
        blocks,
        blocks,
        pltpu.VMEM((8, 3, rows, BLK), BF16),
        pltpu.VMEM((rows, BLK), F32),
        pltpu.SemaphoreType.DMA((16,)),
        pltpu.SemaphoreType.DMA((8, 5)),
        pltpu.SemaphoreType.DMA((8, 3)),
        pltpu.SemaphoreType.DMA((8, 9)),
        pltpu.SemaphoreType.DMA((2,)),
    ]
    out_shape = [struct(rows, 4096)] + [struct(rows, 2048)] * 4
    out_shape += [struct(4, rows, BLK), struct(rows, BLK, dtype=F32)]
    return local_call(
        body, info, operands, out_shape, scratch, 8 * 13 * 2 * rows * BLK * BLK, 22 << 20, aliases
    )


def grads_of(info, half, groups, tokens, mate_tokens, far, mate_far, grad, packed, sums):
    rows = tokens.shape[0]
    pieces = len(far[1])
    jobs, sizes = [], []
    for number, group in enumerate(groups):
        at = 0
        for xr, low, high in group:
            for m in range(low, high):
                jobs.append((number, at, xr, m))
                at += 1
        sizes.append(at)
    used = []
    for _, _, xr, _ in jobs:
        if xr not in used:
            used.append(xr)

    def body(s_ref, t_ref, tm_ref, *rest):
        remote = []
        for i in range(2):
            flat = rest[i * (1 + 2 * pieces) : (i + 1) * (1 + 2 * pieces)]
            remote.append((flat[:1], flat[1 : 1 + pieces], flat[1 + pieces :]))
        rest = rest[2 * (1 + 2 * pieces) :]
        g_ref, x_ref, da_ref, db_ref = rest[:4]
        out_refs = rest[4 : 4 + len(sizes)]
        feed, held, outs, sem_f, sem_h, sem_out = rest[-6:]
        d = s_ref[0]

        def block(xr):
            return (4 * xr + 2 * half) ^ d

        top, bottom = pl.ds(0, rows), pl.ds(rows, rows)

        def grad_pairs(xr, to):
            return [
                (g_ref.at[:, columns(place(block(xr)))], to.at[top]),
                (x_ref.at[xr], to.at[bottom]),
            ]

        shared = []
        for i, xr in enumerate(used):
            for n, (source, to) in enumerate(grad_pairs(xr, held.at[i])):
                shared.append(pltpu.make_async_copy(source, to, sem_h.at[i, n]))
        for n, (source, where) in enumerate(((da_ref, top), (db_ref, bottom))):
            shared.append(
                pltpu.make_async_copy(source, held.at[len(used), where], sem_h.at[len(used), n])
            )

        def reads(n):
            _, _, xr, m = jobs[n]
            if m == 8:
                pairs = grad_pairs(xr, feed.at[n])
            elif m < 5:
                p = columns(block(xr) ^ LOCAL[m][0])
                pairs = [(t_ref.at[:, p], feed.at[n, top]), (tm_ref.at[:, p], feed.at[n, bottom])]
            else:
                p = columns(place(block(xr)))
                pairs = []
                for i in range(2):
                    refs = remote[i][m - 5]
                    tall = rows // len(refs)
                    for q, ref in enumerate(refs):
                        pairs.append((ref.at[:, p], feed.at[n, pl.ds(i * rows + q * tall, tall)]))
            return [pltpu.make_async_copy(a, c, sem_f.at[n]) for a, c in pairs]

        start_all(shared)
        for n in range(len(jobs)):
            start_all(reads(n))
        wait_all(shared)
        slots = [len(used) if m == 8 else used.index(xr) for _, _, xr, m in jobs]
        cut = len(jobs) // 4

        def part(i, carry):
            for q in range(cut):
                whole = feed.at[cut * i + q]
                pltpu.make_async_copy(whole, whole, sem_f.at[cut * i + q]).wait()
            for q in range(cut):
                slot = jnp.where(
                    i < 2,
                    jnp.where(i == 0, slots[q], slots[cut + q]),
                    jnp.where(i == 2, slots[2 * cut + q], slots[3 * cut + q]),
                )
                outs[cut * i + q] = dot_tn(feed[cut * i + q], held[slot]).astype(BF16)
            return carry

        lax.fori_loop(0, 4, part, 0)
        sent = []
        for n, (number, at, _, _) in enumerate(jobs):
            sent.append(pltpu.make_async_copy(outs.at[n], out_refs[number].at[at], sem_out.at[n]))
        start_all(sent)
        wait_all(sent)

    count = len(jobs)
    scratch = [
        pltpu.VMEM((count, 2 * rows, BLK), BF16),
        pltpu.VMEM((len(used) + 1, 2 * rows, BLK), BF16),
        pltpu.VMEM((count, BLK, BLK), BF16),
        pltpu.SemaphoreType.DMA((count,)),
        pltpu.SemaphoreType.DMA((len(used) + 1, 2)),
        pltpu.SemaphoreType.DMA((count,)),
    ]
    return local_call(
        body, info,
        [tokens, mate_tokens, far[0], *far[1], *far[2], mate_far[0], *mate_far[1], *mate_far[2],
         grad, packed, *sums],
        [struct(size, BLK, BLK) for size in sizes], scratch,
        count * 4 * rows * BLK * BLK, count * 3 * 2 * rows * BLK,
    )


def down_grads(info, tokens, mate_tokens, ups):
    rows = tokens.shape[0]

    def body(s_ref, t_ref, tm_ref, ua_ref, ub_ref, *rest):
        out_refs = rest[:4]
        feed, up, outs, sem_f, sem_u, sem_out = rest[4:]
        d = s_ref[0]
        top, bottom = pl.ds(0, rows), pl.ds(rows, rows)
        shared = [
            pltpu.make_async_copy(ua_ref, up.at[top], sem_u.at[0]),
            pltpu.make_async_copy(ub_ref, up.at[bottom], sem_u.at[1]),
        ]

        def reads(n):
            p = columns((2 * n) ^ d)
            return [
                pltpu.make_async_copy(t_ref.at[:, p], feed.at[n, top], sem_f.at[n, 0]),
                pltpu.make_async_copy(tm_ref.at[:, p], feed.at[n, bottom], sem_f.at[n, 1]),
            ]

        start_all(shared)
        for n in range(8):
            start_all(reads(n))
        wait_all(shared)
        sent = []
        for n in range(8):
            wait_all(reads(n))

        def group(base, carry):
            for i in range(4):
                outs[4 * base + i] = dot_tn(feed[4 * base + i], up[...]).astype(BF16)
            return carry

        lax.fori_loop(0, 2, group, 0)
        for n in range(8):
            copy = pltpu.make_async_copy(outs.at[n], out_refs[n // 2].at[n % 2], sem_out.at[n])
            copy.start()
            sent.append(copy)
        wait_all(sent)

    scratch = [
        pltpu.VMEM((8, 2 * rows, BLK), BF16),
        pltpu.VMEM((2 * rows, BLK), BF16),
        pltpu.VMEM((8, BLK, BLK), BF16),
        pltpu.SemaphoreType.DMA((8, 2)),
        pltpu.SemaphoreType.DMA((2,)),
        pltpu.SemaphoreType.DMA((8,)),
    ]
    return local_call(
        body, info, [tokens, mate_tokens, *ups], [struct(2, BLK, BLK)] * 4, scratch,
        8 * 4 * rows * BLK * BLK, 5 << 20,
    )


def back_all(info, grads, weights, up_sum, down_own, down_mate, from_y, from_z):
    rows = grads[0].shape[0]

    def body(s_ref, g0_ref, g1_ref, w_ref, us_ref, *rest):
        d_refs, (y0, y1, z0, z1, out_ref) = rest[:8], rest[8:13]
        g, w, us, dn, ys, zs, outs, sem_in, sem_out, sem_one = rest[13:]
        d = s_ref[0]
        first = pltpu.make_async_copy(us_ref, us, sem_one.at[0])

        def reads(rel):
            half, p = (rel // 2) % 2, columns(place(rel ^ d))
            return [
                pltpu.make_async_copy((g0_ref, g1_ref)[half].at[:, p], g.at[rel], sem_in.at[rel, 0]),
                pltpu.make_async_copy(
                    w_ref.at[rel ^ d, pl.ds(0, 5)], w.at[rel], sem_in.at[rel, 1]
                ),
            ]

        def extras(rel):
            half, p = (rel // 2) % 2, columns(place(rel ^ d))
            return [
                pltpu.make_async_copy(
                    d_refs[4 * (rel % 2) + rel // 4].at[0, (rel // 2) % 2],
                    dn.at[rel],
                    sem_in.at[rel, 2],
                ),
                pltpu.make_async_copy((y0, y1)[half].at[:, p], ys.at[rel], sem_in.at[rel, 3]),
                pltpu.make_async_copy((z0, z1)[half].at[:, p], zs.at[rel], sem_in.at[rel, 4]),
            ]

        first.start()
        for rel in range(16):
            start_all(reads(rel))
            start_all(extras(rel))
        first.wait()
        for rel in range(16):
            wait_all(reads(rel))
            wait_all(extras(rel))

        def write(rel):
            return pltpu.make_async_copy(
                outs.at[rel], out_ref.at[:, columns(rel ^ d)], sem_out.at[rel]
            )

        def group(xr, carry):
            for low in range(4):
                others = [4 * (xr ^ (k // 4)) + (low ^ (k % 4)) for k, _ in LOCAL]
                rel = 4 * xr + low
                fed = jnp.concatenate([g[o] for o in others] + [us[...]], 1)
                rhs = [w[o, level] for o, (_, level) in zip(others, LOCAL)] + [dn[rel]]
                total = dot_nt(fed, jnp.concatenate(rhs, 1))
                total += ys[rel].astype(F32) + zs[rel].astype(F32)
                outs[rel] = total.astype(BF16)
            for low in range(4):
                write(4 * xr + low).start()
            return carry

        lax.fori_loop(0, 4, group, 0)
        for rel in range(16):
            write(rel).wait()

    operands = [*grads, weights, up_sum, *down_own, *down_mate, *from_y, *from_z]
    blocks = pltpu.VMEM((16, rows, BLK), BF16)
    scratch = [
        blocks,
        pltpu.VMEM((16, 5, BLK, BLK), BF16),
        pltpu.VMEM((rows, BLK), BF16),
        blocks,
        blocks,
        blocks,
        blocks,
        pltpu.SemaphoreType.DMA((16, 5)),
        pltpu.SemaphoreType.DMA((16,)),
        pltpu.SemaphoreType.DMA((1,)),
    ]
    return local_call(
        body, info, operands, [struct(rows, 4096)], scratch, 16 * 6 * 2 * rows * BLK * BLK, 22 << 20
    )[0]


def after(values, other):
    return lax.optimization_barrier((tuple(values), other))[0]


def gather_factors(down, up):
    both = jnp.stack([down, up])
    pair = jnp.stack([both, send(both, Y1)], 1)
    own = [pair] + [send(pair, move) for move in (X1, X2, X3)]
    return own, [send(piece, CORE) for piece in own]


def sum_over_mp(part):
    def both(a, b):
        return a.astype(F32) + b.astype(F32)

    pair = both(part, send(part, Y2)).astype(BF16)
    moved = [send(pair, move) for move in (Z1, Z2, Z3)]
    return (both(pair, moved[0]) + both(moved[1], moved[2])).astype(BF16)


def program(tokens, block_weights, lowrank_down, lowrank_up, cotangent, seq_lengths):
    me = lax.axis_index("dp").astype(jnp.int32)
    info = jnp.stack([me, seq_lengths[0]])

    whole_a, low_rows, high_rows, whole_b = take_halves(info, tokens)

    def exchange(whole, parts):
        r6 = [send(part, Z1) for part in parts]
        r7 = [send(part, Z3) for part in r6]
        return send(whole, Y2), r6, r7

    far_a = exchange(whole_a, [low_rows, high_rows])
    far_b = exchange(whole_b, [whole_b])
    factors_own, factors_mate = gather_factors(lowrank_down, lowrank_up)
    mate_tokens = send(tokens, CORE)
    part = down_part(info, tokens, factors_own, factors_mate)
    down_sum = sum_over_mp(part)
    mate_down = send(down_sum, CORE)
    sums = (down_sum, mate_down)

    def to_mate(far):
        return (
            send(far[0], CORE), [send(v, CORE) for v in far[1]], [send(v, CORE) for v in far[2]]
        )

    mate_a, mate_b = to_mate(far_a), to_mate(far_b)

    def forward(half, far, carried):
        output, grad, t5, t6, t7, pack, up = forward_half(
            info, half, tokens, far, block_weights, down_sum, factors_own, factors_mate,
            cotangent, carried,
        )
        pack = send(pack, CORE)
        return output, grad, (t5, t6, t7), pack, up

    def terms_back(terms, other):
        carried = send(terms[2], Z3)
        from_y = send(terms[0], Y2)
        carried = after((carried,), other)[0]
        joined = (terms[1].astype(F32) + carried.astype(F32)).astype(BF16)
        return from_y, send(joined, Z1)

    def local_grads(half, far, mate_far, grad, pack):
        fixed = (tokens, mate_tokens, far, mate_far, grad, pack, sums)
        groups = (((2, 0, 5), (1, 0, 5)), ((2, 5, 9), (3, 5, 9)), ((1, 5, 9),), ((3, 0, 5),))
        groups += (((0, 0, 5),), ((0, 5, 9),))
        made = grads_of(info, half, groups, *fixed)
        return made[:2], made[2:]

    def over_x(gone, rest, extra, other):
        to1, to3 = gone
        late1, late3, own_low, own_high = rest
        got1 = send(to1, X1)
        got3 = send(to3, X3)
        got1, got3 = after((got1, got3), other)
        late1 = (late1.astype(F32) + got3[:4].astype(F32)).astype(BF16)
        late3 = (late3.astype(F32) + got1[:5].astype(F32)).astype(BF16)
        if extra:
            late1 = jnp.concatenate([late1, extra[0]])
            late3 = jnp.concatenate([late3, extra[1]])
        end1 = send(late1, X1)
        end3 = send(late3, X3)
        return got1, got3, end1, end3, own_low, own_high

    def finish(parts, other):
        got1, got3, end1, end3, own_low, own_high = parts
        end1, end3 = after((end1, end3), other)
        low = own_low.astype(F32) + got1[5:].astype(F32) + end3[:5].astype(F32)
        high = own_high.astype(F32) + got3[4:].astype(F32) + end1[:4].astype(F32)
        return low, high, end1[4:], end3[5:]

    output, grad_a, terms_a, pack_a, up_a = forward(1, far_a, None)
    gone_a, rest_a = local_grads(1, far_a, mate_a, grad_a, pack_a)
    y_a, z_a = terms_back(terms_a, rest_a[0])

    output, grad_b, terms_b, pack_b, up_b = forward(0, far_b, output)
    x_a = over_x(gone_a, rest_a, None, up_b)
    gone_b, rest_b = local_grads(0, far_b, mate_b, grad_b, pack_b)
    y_b, z_b = terms_back(terms_b, rest_b[0])
    low_a, high_a, _, _ = finish(x_a, rest_b[0])
    across = send(jnp.concatenate([low_a, high_a]).astype(BF16), Y1)

    up_sum = sum_over_mp((up_a + up_b).astype(BF16))
    mate_up = send(up_sum, CORE)
    d0, d1, d2, d3 = down_grads(info, tokens, mate_tokens, (up_sum, mate_up))
    d2 = send(d2, X2)
    x_b = over_x(gone_b, rest_b, (d1, d3), d0)
    grad_tokens = back_all(
        info, (grad_b, grad_a), block_weights, up_sum, factors_own, factors_mate,
        (y_b, y_a), (z_b, z_a),
    )
    low_b, high_b, d1, d3 = finish(x_b, grad_tokens)
    across, d2 = after((across, d2), grad_tokens)
    downs = d0.astype(F32) + d1.astype(F32) + d2.astype(F32) + d3.astype(F32)
    grad_down = (downs[0] + send(downs[1].astype(BF16), Y1).astype(F32)).astype(BF16)
    grad_low = low_b + across[:5].astype(F32)
    grad_high = high_b + across[5:].astype(F32)
    grad_blocks = jnp.concatenate([grad_low, grad_high[:3]]).astype(BF16)[None]
    grad_lowrank = jnp.stack([grad_down, grad_high[3].astype(BF16)], 1)
    return (output, grad_tokens, grad_blocks, grad_lowrank)


def solution(mesh):
    placed = (
        P("dp", "mp"),
        P("mp", None, None, None),
        P(("mp", "dp"), None),
        P(("mp", "dp"), None),
        P("dp", "mp"),
        P("dp"),
    )
    return jax.shard_map(
        program,
        mesh=mesh,
        in_specs=placed,
        out_specs=(
            P("dp", "mp"),
            P("dp", "mp"),
            P(("mp", "dp"), None, None, None),
            P(("mp", "dp"), None, None),
        ),
        check_vma=False,
    )
```

```python
import jax
import jax.numpy as jnp
from jax import lax
from jax.experimental import pallas as pl
from jax.experimental.pallas import tpu as pltpu
from jax.sharding import PartitionSpec as P


F32, BF16 = jnp.float32, jnp.bfloat16
BLK = 256
CORE, Y1, X1, X2, X3 = (1, 0), (2, 0), (4, 0), (8, 0), (12, 0)
Y2, Z1, Z2, Z3 = (0, 1), (0, 2), (0, 4), (0, 6)
LOCAL = ((0, 0), (1, 1), (2, 2), (4, 3), (8, 4))


def send(value, move):
    ways = lax.axis_size("mp")
    mask = move[0] * ways + move[1]
    total = lax.axis_size("dp") * ways
    return lax.ppermute(value, ("dp", "mp"), [(s, s ^ mask) for s in range(total)])


def dot(a, b):
    return jnp.dot(a, b, preferred_element_type=F32)


def dot_nt(a, b):
    return lax.dot_general(a, b, (((1,), (1,)), ((), ())), preferred_element_type=F32)


def dot_tn(a, b):
    return lax.dot_general(a, b, (((0,), (0,)), ((), ())), preferred_element_type=F32)


def place(b):
    return (b // 4) * 2 + b % 2


def cost(flops, moved):
    return pl.CostEstimate(flops=flops, bytes_accessed=moved, transcendentals=0)


def struct(*shape, dtype=BF16):
    return jax.ShapeDtypeStruct(shape, dtype)


def local_call(body, info, operands, out_shape, scratch, flops, moved, aliases=None):
    anywhere = pl.BlockSpec(memory_space=pl.ANY)
    return pl.pallas_call(
        body,
        in_specs=[pl.BlockSpec(memory_space=pltpu.SMEM)] + [anywhere] * len(operands),
        out_specs=[anywhere] * len(out_shape),
        out_shape=out_shape,
        scratch_shapes=scratch,
        input_output_aliases=aliases or {},
        cost_estimate=cost(flops, moved),
    )(info, *operands)


def columns(index, width=BLK):
    return pl.ds(pl.multiple_of(index * width, width), width)


def take_halves(info, tokens):
    rows = tokens.shape[0]
    height = rows // 2

    def body(s_ref, t_ref, a_ref, p0_ref, p1_ref, b_ref, buf, sems):
        own = (s_ref[0] // 2) % 2

        def read(half, x):
            piece = columns(2 * x + (own ^ half), 512)
            return pltpu.make_async_copy(t_ref.at[:, piece], buf.at[half, x], sems.at[0, half, x])

        def writes(half, x):
            to = pl.ds(512 * x, 512)
            if not half:
                return [pltpu.make_async_copy(buf.at[0, x], b_ref.at[:, to], sems.at[1, 0, x])]
            pairs = [(buf.at[1, x], a_ref)]
            pairs.append((buf.at[1, x, pl.ds(0, height)], p0_ref))
            pairs.append((buf.at[1, x, pl.ds(height, height)], p1_ref))
            return [
                pltpu.make_async_copy(a, ref.at[:, to], sems.at[1 + i, 1, x])
                for i, (a, ref) in enumerate(pairs)
            ]

        steps = [(half, x) for half in (1, 0) for x in range(4)]
        for step in steps:
            read(*step).start()
        sent = []
        for step in steps:
            read(*step).wait()
            sent += writes(*step)
            start_all(writes(*step))
        wait_all(sent)

    scratch = [pltpu.VMEM((2, 4, rows, 512), BF16), pltpu.SemaphoreType.DMA((4, 2, 4))]
    out_shape = [struct(rows, 2048), struct(height, 2048), struct(height, 2048), struct(rows, 2048)]
    return local_call(body, info, [tokens], out_shape, scratch, 0, 10 * rows * 2048)


def down_part(info, tokens, own, mate):
    rows = tokens.shape[0]

    def body(s_ref, t_ref, *rest):
        f_refs, (o_ref, t, f, o, sems) = rest[:8], rest[8:]
        d = s_ref[0]
        reads = [pltpu.make_async_copy(t_ref, t, sems.at[8])]
        for i, ref in enumerate(f_refs):
            reads.append(pltpu.make_async_copy(ref.at[0], f.at[i], sems.at[i]))
        for read in reads:
            read.start()
        for read in reads:
            read.wait()
        total = jnp.zeros((rows, BLK), F32)
        for i in range(8):
            for low in range(2):
                rel = 4 * (i % 4) + 2 * low + i // 4
                total += dot(t[:, columns(rel ^ d)], f[i, low])
        o[...] = total.astype(BF16)
        write = pltpu.make_async_copy(o, o_ref, sems.at[9])
        write.start()
        write.wait()

    scratch = [
        pltpu.VMEM((rows, 4096), BF16),
        pltpu.VMEM((8, 2, BLK, BLK), BF16),
        pltpu.VMEM((rows, BLK), BF16),
        pltpu.SemaphoreType.DMA((10,)),
    ]
    return local_call(
        body, info, [tokens, *own, *mate], [struct(rows, BLK)], scratch,
        2 * rows * 4096 * BLK, 2 * (rows * 4096 + 4096 * BLK),
    )[0]


def start_all(copies):
    for copy in copies:
        copy.start()


def wait_all(copies):
    for copy in copies:
        copy.wait()


def forward_half(info, half, tokens, far, weights, down_sum, up_own, up_mate, cotangent, carried):
    rows = tokens.shape[0]
    pieces = len(far[1])
    height = rows // pieces

    def body(s_ref, t_ref, r5_ref, *rest):
        r6_refs, r7_refs = rest[:pieces], rest[pieces : 2 * pieces]
        w_ref, ds_ref = rest[2 * pieces : 2 * pieces + 2]
        u_refs = rest[2 * pieces + 2 : 2 * pieces + 10]
        ct_ref = rest[2 * pieces + 10]
        (out_ref, g_ref, o5_ref, o6_ref, o7_ref, x_ref, up_ref,
         t, r, w, ds, u, ct, outs, gs, gone, part, sem_t, sem_r, sem_in, sem_out, sem_one) = rest[-22:]
        d, alive = s_ref[0], s_ref[1]

        def rel_of(j):
            return 4 * (j // 2) + 2 * half + j % 2

        def spot(j):
            return columns(place(rel_of(j) ^ d))

        token_reads = [
            pltpu.make_async_copy(t_ref.at[:, columns(rel ^ d)], t.at[rel], sem_t.at[rel])
            for rel in range(16)
        ]
        first = pltpu.make_async_copy(ds_ref, ds, sem_one.at[0])

        def reads(j, parity):
            b = rel_of(j) ^ d
            factor = u_refs[4 * parity + j // 2 if isinstance(j, int) else 0]
            copies = [
                pltpu.make_async_copy(w_ref.at[b], w.at[j], sem_in.at[j, 0]),
                pltpu.make_async_copy(ct_ref.at[:, columns(b)], ct.at[j], sem_in.at[j, 1]),
                pltpu.make_async_copy(factor.at[1, half], u.at[j], sem_in.at[j, 2]),
                pltpu.make_async_copy(r5_ref.at[:, spot(j)], r.at[j, 0], sem_r.at[j, 0]),
            ]
            for p in range(pieces):
                for i, refs in ((1, r6_refs), (2, r7_refs)):
                    copies.append(
                        pltpu.make_async_copy(
                            refs[p].at[:, spot(j)],
                            r.at[j, i, pl.ds(p * height, height)],
                            sem_r.at[j, 1 + 2 * p + i - 1],
                        )
                    )
            return copies

        def writes(j, parity):
            b = rel_of(j) ^ d
            pairs = [(outs.at[j], out_ref.at[:, columns(b)]), (gs.at[j], g_ref.at[:, spot(j)])]
            for i, ref in enumerate((o5_ref, o6_ref, o7_ref)):
                pairs.append((gone.at[j, i], ref.at[:, spot(j)]))
            if parity:
                pairs.append((gs.at[j], x_ref.at[j // 2]))
            return [pltpu.make_async_copy(a, c, sem_out.at[j, i]) for i, (a, c) in enumerate(pairs)]

        first.start()
        start_all(token_reads)
        for j in range(8):
            start_all(reads(j, j % 2))
        first.wait()
        wait_all(token_reads)

        def group(base, carry):
            js = [4 * base + i for i in range(4)]
            for i, j in enumerate(js):
                wait_all(reads(j, i % 2))
            live = lax.broadcasted_iota(jnp.int32, (rows, BLK), 0) < alive
            scale = 0.7978845608028654
            for i, j in enumerate(js):
                within = 4 * (i // 2) + 2 * half + i % 2
                fed = [t[8 * (base ^ (k // 8)) + (within ^ (k % 8))] for k, _ in LOCAL]
                fed += [r[j, n] for n in range(3)]
                hidden = dot(jnp.concatenate(fed, 1), w[j].reshape(8 * BLK, BLK))
                hidden += dot_nt(ds[...], u[j])
                square = hidden * hidden
                bent = jnp.tanh(scale * hidden * (1.0 + 0.044715 * square))
                up = 0.5 * (1.0 + bent)
                slope = up + 0.5 * hidden * (1.0 - bent * bent) * scale * (1.0 + 0.134145 * square)
                outs[j] = jnp.where(live, hidden * up, 0.0).astype(BF16)
                gs[j] = jnp.where(live, ct[j].astype(F32) * slope, 0.0).astype(BF16)
            for j in js:
                back = dot_nt(gs[j], w[j, 5:8].reshape(3 * BLK, BLK)).astype(BF16)
                for i in range(3):
                    gone[j, i] = back[:, i * BLK : (i + 1) * BLK]
            grads = jnp.concatenate([gs[j] for j in js], 1)
            factors = jnp.concatenate([u[j] for j in js], 0)
            part[...] = jnp.where(base == 0, 0.0, part[...]) + dot(grads, factors)
            for i, j in enumerate(js):
                start_all(writes(j, i % 2))
            return carry

        part[...] = jnp.zeros_like(part)
        lax.fori_loop(0, 2, group, 0)
        sent = []
        for j in range(8):
            sent += writes(j, j % 2)
        last = pltpu.make_async_copy(part, up_ref, sem_one.at[1])
        last.start()
        wait_all(sent)
        last.wait()

    operands = [tokens, far[0], *far[1], *far[2], weights, down_sum, *up_own, *up_mate, cotangent]
    aliases = {}
    if carried is not None:
        aliases = {len(operands) + 1: 0}
        operands.append(carried)
    blocks = pltpu.VMEM((8, rows, BLK), BF16)
    scratch = [
        pltpu.VMEM((16, rows, BLK), BF16),
        pltpu.VMEM((8, 3, rows, BLK), BF16),
        pltpu.VMEM((8, 8, BLK, BLK), BF16),
        pltpu.VMEM((rows, BLK), BF16),
        blocks,
        blocks,
        blocks,
        blocks,
        pltpu.VMEM((8, 3, rows, BLK), BF16),
        pltpu.VMEM((rows, BLK), F32),
        pltpu.SemaphoreType.DMA((16,)),
        pltpu.SemaphoreType.DMA((8, 5)),
        pltpu.SemaphoreType.DMA((8, 3)),
        pltpu.SemaphoreType.DMA((8, 9)),
        pltpu.SemaphoreType.DMA((2,)),
    ]
    out_shape = [struct(rows, 4096)] + [struct(rows, 2048)] * 4
    out_shape += [struct(4, rows, BLK), struct(rows, BLK, dtype=F32)]
    return local_call(
        body, info, operands, out_shape, scratch, 8 * 13 * 2 * rows * BLK * BLK, 22 << 20, aliases
    )


def grads_of(info, half, groups, tokens, mate_tokens, far, mate_far, grad, packed, sums):
    rows = tokens.shape[0]
    pieces = len(far[1])
    jobs, sizes = [], []
    for number, group in enumerate(groups):
        at = 0
        for xr, low, high in group:
            for m in range(low, high):
                jobs.append((number, at, xr, m))
                at += 1
        sizes.append(at)
    used = []
    for _, _, xr, _ in jobs:
        if xr not in used:
            used.append(xr)

    def body(s_ref, t_ref, tm_ref, *rest):
        remote = []
        for i in range(2):
            flat = rest[i * (1 + 2 * pieces) : (i + 1) * (1 + 2 * pieces)]
            remote.append((flat[:1], flat[1 : 1 + pieces], flat[1 + pieces :]))
        rest = rest[2 * (1 + 2 * pieces) :]
        g_ref, x_ref, da_ref, db_ref = rest[:4]
        out_refs = rest[4 : 4 + len(sizes)]
        feed, held, outs, sem_f, sem_h, sem_out = rest[-6:]
        d = s_ref[0]

        def block(xr):
            return (4 * xr + 2 * half) ^ d

        top, bottom = pl.ds(0, rows), pl.ds(rows, rows)

        def grad_pairs(xr, to):
            return [
                (g_ref.at[:, columns(place(block(xr)))], to.at[top]),
                (x_ref.at[xr], to.at[bottom]),
            ]

        shared = []
        for i, xr in enumerate(used):
            for n, (source, to) in enumerate(grad_pairs(xr, held.at[i])):
                shared.append(pltpu.make_async_copy(source, to, sem_h.at[i, n]))
        for n, (source, where) in enumerate(((da_ref, top), (db_ref, bottom))):
            shared.append(
                pltpu.make_async_copy(source, held.at[len(used), where], sem_h.at[len(used), n])
            )

        def reads(n):
            _, _, xr, m = jobs[n]
            if m == 8:
                pairs = grad_pairs(xr, feed.at[n])
            elif m < 5:
                p = columns(block(xr) ^ LOCAL[m][0])
                pairs = [(t_ref.at[:, p], feed.at[n, top]), (tm_ref.at[:, p], feed.at[n, bottom])]
            else:
                p = columns(place(block(xr)))
                pairs = []
                for i in range(2):
                    refs = remote[i][m - 5]
                    tall = rows // len(refs)
                    for q, ref in enumerate(refs):
                        pairs.append((ref.at[:, p], feed.at[n, pl.ds(i * rows + q * tall, tall)]))
            return [pltpu.make_async_copy(a, c, sem_f.at[n]) for a, c in pairs]

        start_all(shared)
        for n in range(len(jobs)):
            start_all(reads(n))
        wait_all(shared)
        slots = [len(used) if m == 8 else used.index(xr) for _, _, xr, m in jobs]
        cut = len(jobs) // 4

        def part(i, carry):
            for q in range(cut):
                whole = feed.at[cut * i + q]
                pltpu.make_async_copy(whole, whole, sem_f.at[cut * i + q]).wait()
            for q in range(cut):
                slot = jnp.where(
                    i < 2,
                    jnp.where(i == 0, slots[q], slots[cut + q]),
                    jnp.where(i == 2, slots[2 * cut + q], slots[3 * cut + q]),
                )
                outs[cut * i + q] = dot_tn(feed[cut * i + q], held[slot]).astype(BF16)
            return carry

        lax.fori_loop(0, 4, part, 0)
        sent = []
        for n, (number, at, _, _) in enumerate(jobs):
            sent.append(pltpu.make_async_copy(outs.at[n], out_refs[number].at[at], sem_out.at[n]))
        start_all(sent)
        wait_all(sent)

    count = len(jobs)
    scratch = [
        pltpu.VMEM((count, 2 * rows, BLK), BF16),
        pltpu.VMEM((len(used) + 1, 2 * rows, BLK), BF16),
        pltpu.VMEM((count, BLK, BLK), BF16),
        pltpu.SemaphoreType.DMA((count,)),
        pltpu.SemaphoreType.DMA((len(used) + 1, 2)),
        pltpu.SemaphoreType.DMA((count,)),
    ]
    return local_call(
        body, info,
        [tokens, mate_tokens, far[0], *far[1], *far[2], mate_far[0], *mate_far[1], *mate_far[2],
         grad, packed, *sums],
        [struct(size, BLK, BLK) for size in sizes], scratch,
        count * 4 * rows * BLK * BLK, count * 3 * 2 * rows * BLK,
    )


def down_grads(info, tokens, mate_tokens, ups):
    rows = tokens.shape[0]

    def body(s_ref, t_ref, tm_ref, ua_ref, ub_ref, *rest):
        out_refs = rest[:4]
        feed, up, outs, sem_f, sem_u, sem_out = rest[4:]
        d = s_ref[0]
        top, bottom = pl.ds(0, rows), pl.ds(rows, rows)
        shared = [
            pltpu.make_async_copy(ua_ref, up.at[top], sem_u.at[0]),
            pltpu.make_async_copy(ub_ref, up.at[bottom], sem_u.at[1]),
        ]

        def reads(n):
            p = columns((2 * n) ^ d)
            return [
                pltpu.make_async_copy(t_ref.at[:, p], feed.at[n, top], sem_f.at[n, 0]),
                pltpu.make_async_copy(tm_ref.at[:, p], feed.at[n, bottom], sem_f.at[n, 1]),
            ]

        start_all(shared)
        for n in range(8):
            start_all(reads(n))
        wait_all(shared)
        sent = []
        for n in range(8):
            wait_all(reads(n))

        def group(base, carry):
            for i in range(4):
                outs[4 * base + i] = dot_tn(feed[4 * base + i], up[...]).astype(BF16)
            return carry

        lax.fori_loop(0, 2, group, 0)
        for n in range(8):
            copy = pltpu.make_async_copy(outs.at[n], out_refs[n // 2].at[n % 2], sem_out.at[n])
            copy.start()
            sent.append(copy)
        wait_all(sent)

    scratch = [
        pltpu.VMEM((8, 2 * rows, BLK), BF16),
        pltpu.VMEM((2 * rows, BLK), BF16),
        pltpu.VMEM((8, BLK, BLK), BF16),
        pltpu.SemaphoreType.DMA((8, 2)),
        pltpu.SemaphoreType.DMA((2,)),
        pltpu.SemaphoreType.DMA((8,)),
    ]
    return local_call(
        body, info, [tokens, mate_tokens, *ups], [struct(2, BLK, BLK)] * 4, scratch,
        8 * 4 * rows * BLK * BLK, 5 << 20,
    )


def back_all(info, grads, weights, up_sum, down_own, down_mate, from_y, from_z):
    rows = grads[0].shape[0]

    def body(s_ref, g0_ref, g1_ref, w_ref, us_ref, *rest):
        d_refs, (y0, y1, z0, z1, out_ref) = rest[:8], rest[8:13]
        g, w, us, dn, ys, zs, outs, sem_in, sem_out, sem_one = rest[13:]
        d = s_ref[0]
        first = pltpu.make_async_copy(us_ref, us, sem_one.at[0])

        def reads(rel):
            half, p = (rel // 2) % 2, columns(place(rel ^ d))
            return [
                pltpu.make_async_copy((g0_ref, g1_ref)[half].at[:, p], g.at[rel], sem_in.at[rel, 0]),
                pltpu.make_async_copy(
                    w_ref.at[rel ^ d, pl.ds(0, 5)], w.at[rel], sem_in.at[rel, 1]
                ),
            ]

        def extras(rel):
            half, p = (rel // 2) % 2, columns(place(rel ^ d))
            return [
                pltpu.make_async_copy(
                    d_refs[4 * (rel % 2) + rel // 4].at[0, (rel // 2) % 2],
                    dn.at[rel],
                    sem_in.at[rel, 2],
                ),
                pltpu.make_async_copy((y0, y1)[half].at[:, p], ys.at[rel], sem_in.at[rel, 3]),
                pltpu.make_async_copy((z0, z1)[half].at[:, p], zs.at[rel], sem_in.at[rel, 4]),
            ]

        first.start()
        for rel in range(16):
            start_all(reads(rel))
            start_all(extras(rel))
        first.wait()
        for rel in range(16):
            wait_all(reads(rel))
            wait_all(extras(rel))

        def write(rel):
            return pltpu.make_async_copy(
                outs.at[rel], out_ref.at[:, columns(rel ^ d)], sem_out.at[rel]
            )

        def group(xr, carry):
            for low in range(4):
                others = [4 * (xr ^ (k // 4)) + (low ^ (k % 4)) for k, _ in LOCAL]
                rel = 4 * xr + low
                fed = jnp.concatenate([g[o] for o in others] + [us[...]], 1)
                rhs = [w[o, level] for o, (_, level) in zip(others, LOCAL)] + [dn[rel]]
                total = dot_nt(fed, jnp.concatenate(rhs, 1))
                total += ys[rel].astype(F32) + zs[rel].astype(F32)
                outs[rel] = total.astype(BF16)
            for low in range(4):
                write(4 * xr + low).start()
            return carry

        lax.fori_loop(0, 4, group, 0)
        for rel in range(16):
            write(rel).wait()

    operands = [*grads, weights, up_sum, *down_own, *down_mate, *from_y, *from_z]
    blocks = pltpu.VMEM((16, rows, BLK), BF16)
    scratch = [
        blocks,
        pltpu.VMEM((16, 5, BLK, BLK), BF16),
        pltpu.VMEM((rows, BLK), BF16),
        blocks,
        blocks,
        blocks,
        blocks,
        pltpu.SemaphoreType.DMA((16, 5)),
        pltpu.SemaphoreType.DMA((16,)),
        pltpu.SemaphoreType.DMA((1,)),
    ]
    return local_call(
        body, info, operands, [struct(rows, 4096)], scratch, 16 * 6 * 2 * rows * BLK * BLK, 22 << 20
    )[0]


def after(values, other):
    return lax.optimization_barrier((tuple(values), other))[0]


def gather_factors(down, up):
    both = jnp.stack([down, up])
    pair = jnp.stack([both, send(both, Y1)], 1)
    own = [pair] + [send(pair, move) for move in (X1, X2, X3)]
    return own, [send(piece, CORE) for piece in own]


def sum_over_mp(part):
    def both(a, b):
        return a.astype(F32) + b.astype(F32)

    pair = both(part, send(part, Y2)).astype(BF16)
    moved = [send(pair, move) for move in (Z1, Z2, Z3)]
    return (both(pair, moved[0]) + both(moved[1], moved[2])).astype(BF16)


def program(tokens, block_weights, lowrank_down, lowrank_up, cotangent, seq_lengths):
    me = lax.axis_index("dp").astype(jnp.int32)
    info = jnp.stack([me, seq_lengths[0]])

    whole_a, low_rows, high_rows, whole_b = take_halves(info, tokens)

    def exchange(whole, parts):
        r6 = [send(part, Z1) for part in parts]
        r7 = [send(part, Z3) for part in r6]
        return send(whole, Y2), r6, r7

    far_a = exchange(whole_a, [low_rows, high_rows])
    far_b = exchange(whole_b, [whole_b])
    factors_own, factors_mate = gather_factors(lowrank_down, lowrank_up)
    mate_tokens = send(tokens, CORE)
    part = down_part(info, tokens, factors_own, factors_mate)
    down_sum = sum_over_mp(part)
    mate_down = send(down_sum, CORE)
    sums = (down_sum, mate_down)

    def to_mate(far):
        return (
            send(far[0], CORE), [send(v, CORE) for v in far[1]], [send(v, CORE) for v in far[2]]
        )

    mate_a, mate_b = to_mate(far_a), to_mate(far_b)

    def forward(half, far, carried):
        output, grad, t5, t6, t7, pack, up = forward_half(
            info, half, tokens, far, block_weights, down_sum, factors_own, factors_mate,
            cotangent, carried,
        )
        pack = send(pack, CORE)
        return output, grad, (t5, t6, t7), pack, up

    def terms_back(terms, other):
        carried = send(terms[2], Z3)
        from_y = send(terms[0], Y2)
        carried = after((carried,), other)[0]
        joined = (terms[1].astype(F32) + carried.astype(F32)).astype(BF16)
        return from_y, send(joined, Z1)

    def local_grads(half, far, mate_far, grad, pack):
        fixed = (tokens, mate_tokens, far, mate_far, grad, pack, sums)
        groups = (((2, 0, 5), (1, 0, 5)), ((2, 5, 9), (3, 5, 9)), ((1, 5, 9),), ((3, 0, 5),))
        groups += (((0, 0, 5),), ((0, 5, 9),))
        made = grads_of(info, half, groups, *fixed)
        return made[:2], made[2:]

    def over_x(gone, rest, extra, other):
        to1, to3 = gone
        late1, late3, own_low, own_high = rest
        got1 = send(to1, X1)
        got3 = send(to3, X3)
        got1, got3 = after((got1, got3), other)
        late1 = (late1.astype(F32) + got3[:4].astype(F32)).astype(BF16)
        late3 = (late3.astype(F32) + got1[:5].astype(F32)).astype(BF16)
        if extra:
            late1 = jnp.concatenate([late1, extra[0]])
            late3 = jnp.concatenate([late3, extra[1]])
        end1 = send(late1, X1)
        end3 = send(late3, X3)
        return got1, got3, end1, end3, own_low, own_high

    def finish(parts, other):
        got1, got3, end1, end3, own_low, own_high = parts
        end1, end3 = after((end1, end3), other)
        low = own_low.astype(F32) + got1[5:].astype(F32) + end3[:5].astype(F32)
        high = own_high.astype(F32) + got3[4:].astype(F32) + end1[:4].astype(F32)
        return low, high

    output, grad_a, terms_a, pack_a, up_a = forward(1, far_a, None)
    gone_a, rest_a = local_grads(1, far_a, mate_a, grad_a, pack_a)
    y_a, z_a = terms_back(terms_a, rest_a[0])

    output, grad_b, terms_b, pack_b, up_b = forward(0, far_b, output)
    x_a = over_x(gone_a, rest_a, None, up_b)
    gone_b, rest_b = local_grads(0, far_b, mate_b, grad_b, pack_b)
    y_b, z_b = terms_back(terms_b, rest_b[0])
    low_a, high_a = finish(x_a, rest_b[0])
    across = send(jnp.concatenate([low_a, high_a]).astype(BF16), Y1)

    up_sum = sum_over_mp((up_a + up_b).astype(BF16))
    mate_up = send(up_sum, CORE)
    d0, d1, d2, d3 = down_grads(info, tokens, mate_tokens, (up_sum, mate_up))
    d2 = send(d2, X2)
    x_b = over_x(gone_b, rest_b, (d1, d3), d0)
    grad_tokens = back_all(
        info, (grad_b, grad_a), block_weights, up_sum, factors_own, factors_mate,
        (y_b, y_a), (z_b, z_a),
    )
    d1, d3 = x_b[2][4:], x_b[3][5:]
    d1, d2, d3 = after((d1, d2, d3), grad_tokens)
    downs = d0.astype(F32) + d1.astype(F32) + d2.astype(F32) + d3.astype(F32)
    sent_down = downs[1].astype(BF16)
    grad_down = (downs[0] + send(sent_down, Y1).astype(F32)).astype(BF16)
    low_b, high_b = finish(x_b, sent_down)
    across = after((across,), sent_down)[0]
    grad_low = low_b + across[:5].astype(F32)
    grad_high = high_b + across[5:].astype(F32)
    grad_blocks = jnp.concatenate([grad_low, grad_high[:3]]).astype(BF16)[None]
    grad_lowrank = jnp.stack([grad_down, grad_high[3].astype(BF16)], 1)
    return (output, grad_tokens, grad_blocks, grad_lowrank)


def solution(mesh):
    placed = (
        P("dp", "mp"),
        P("mp", None, None, None),
        P(("mp", "dp"), None),
        P(("mp", "dp"), None),
        P("dp", "mp"),
        P("dp"),
    )
    return jax.shard_map(
        program,
        mesh=mesh,
        in_specs=placed,
        out_specs=(
            P("dp", "mp"),
            P("dp", "mp"),
            P(("mp", "dp"), None, None, None),
            P(("mp", "dp"), None, None),
        ),
        check_vma=False,
    )
```

```python
import jax
import jax.numpy as jnp
from jax import lax
from jax.experimental import pallas as pl
from jax.experimental.pallas import tpu as pltpu
from jax.sharding import PartitionSpec as P


F32, BF16 = jnp.float32, jnp.bfloat16
BLK = 256
CORE, Y1, X1, X2, X3 = (1, 0), (2, 0), (4, 0), (8, 0), (12, 0)
Y2, Z1, Z2, Z3 = (0, 1), (0, 2), (0, 4), (0, 6)
LOCAL = ((0, 0), (1, 1), (2, 2), (4, 3), (8, 4))


def send(value, move):
    ways = lax.axis_size("mp")
    mask = move[0] * ways + move[1]
    total = lax.axis_size("dp") * ways
    return lax.ppermute(value, ("dp", "mp"), [(s, s ^ mask) for s in range(total)])


def dot(a, b):
    return jnp.dot(a, b, preferred_element_type=F32)


def dot_nt(a, b):
    return lax.dot_general(a, b, (((1,), (1,)), ((), ())), preferred_element_type=F32)


def dot_tn(a, b):
    return lax.dot_general(a, b, (((0,), (0,)), ((), ())), preferred_element_type=F32)


def place(b):
    return (b // 4) * 2 + b % 2


def cost(flops, moved):
    return pl.CostEstimate(flops=flops, bytes_accessed=moved, transcendentals=0)


def struct(*shape, dtype=BF16):
    return jax.ShapeDtypeStruct(shape, dtype)


def local_call(body, info, operands, out_shape, scratch, flops, moved, aliases=None):
    anywhere = pl.BlockSpec(memory_space=pl.ANY)
    return pl.pallas_call(
        body,
        in_specs=[pl.BlockSpec(memory_space=pltpu.SMEM)] + [anywhere] * len(operands),
        out_specs=[anywhere] * len(out_shape),
        out_shape=out_shape,
        scratch_shapes=scratch,
        input_output_aliases=aliases or {},
        cost_estimate=cost(flops, moved),
    )(info, *operands)


def columns(index, width=BLK):
    return pl.ds(pl.multiple_of(index * width, width), width)


def take_halves(info, tokens):
    rows = tokens.shape[0]
    height = rows // 2

    def body(s_ref, t_ref, a_ref, p0_ref, p1_ref, b_ref, buf, sems):
        own = (s_ref[0] // 2) % 2

        def read(half, x):
            piece = columns(2 * x + (own ^ half), 512)
            return pltpu.make_async_copy(t_ref.at[:, piece], buf.at[half, x], sems.at[0, half, x])

        def writes(half, x):
            to = pl.ds(512 * x, 512)
            if not half:
                return [pltpu.make_async_copy(buf.at[0, x], b_ref.at[:, to], sems.at[1, 0, x])]
            pairs = [(buf.at[1, x], a_ref)]
            pairs.append((buf.at[1, x, pl.ds(0, height)], p0_ref))
            pairs.append((buf.at[1, x, pl.ds(height, height)], p1_ref))
            return [
                pltpu.make_async_copy(a, ref.at[:, to], sems.at[1 + i, 1, x])
                for i, (a, ref) in enumerate(pairs)
            ]

        steps = [(half, x) for half in (1, 0) for x in range(4)]
        for step in steps:
            read(*step).start()
        sent = []
        for step in steps:
            read(*step).wait()
            sent += writes(*step)
            start_all(writes(*step))
        wait_all(sent)

    scratch = [pltpu.VMEM((2, 4, rows, 512), BF16), pltpu.SemaphoreType.DMA((4, 2, 4))]
    out_shape = [struct(rows, 2048), struct(height, 2048), struct(height, 2048), struct(rows, 2048)]
    return local_call(body, info, [tokens], out_shape, scratch, 0, 10 * rows * 2048)


def down_part(info, tokens, own, mate):
    rows = tokens.shape[0]

    def body(s_ref, t_ref, *rest):
        f_refs, (o_ref, t, f, o, sems) = rest[:8], rest[8:]
        d = s_ref[0]
        reads = [pltpu.make_async_copy(t_ref, t, sems.at[8])]
        for i, ref in enumerate(f_refs):
            reads.append(pltpu.make_async_copy(ref.at[0], f.at[i], sems.at[i]))
        for read in reads:
            read.start()
        for read in reads:
            read.wait()
        total = jnp.zeros((rows, BLK), F32)
        for i in range(8):
            for low in range(2):
                rel = 4 * (i % 4) + 2 * low + i // 4
                total += dot(t[:, columns(rel ^ d)], f[i, low])
        o[...] = total.astype(BF16)
        write = pltpu.make_async_copy(o, o_ref, sems.at[9])
        write.start()
        write.wait()

    scratch = [
        pltpu.VMEM((rows, 4096), BF16),
        pltpu.VMEM((8, 2, BLK, BLK), BF16),
        pltpu.VMEM((rows, BLK), BF16),
        pltpu.SemaphoreType.DMA((10,)),
    ]
    return local_call(
        body, info, [tokens, *own, *mate], [struct(rows, BLK)], scratch,
        2 * rows * 4096 * BLK, 2 * (rows * 4096 + 4096 * BLK),
    )[0]


def start_all(copies):
    for copy in copies:
        copy.start()


def wait_all(copies):
    for copy in copies:
        copy.wait()


def forward_half(info, half, tokens, far, weights, down_sum, up_own, up_mate, cotangent, carried):
    rows = tokens.shape[0]
    pieces = len(far[1])
    height = rows // pieces

    def body(s_ref, t_ref, r5_ref, *rest):
        r6_refs, r7_refs = rest[:pieces], rest[pieces : 2 * pieces]
        w_ref, ds_ref = rest[2 * pieces : 2 * pieces + 2]
        u_refs = rest[2 * pieces + 2 : 2 * pieces + 10]
        ct_ref = rest[2 * pieces + 10]
        (out_ref, g_ref, o5_ref, o6_ref, o7_ref, x_ref, up_ref,
         t, r, w, ds, u, ct, outs, gs, gone, part, sem_t, sem_r, sem_in, sem_out, sem_one) = rest[-22:]
        d, alive = s_ref[0], s_ref[1]

        def rel_of(j):
            return 4 * (j // 2) + 2 * half + j % 2

        def spot(j):
            return columns(place(rel_of(j) ^ d))

        token_reads = [
            pltpu.make_async_copy(t_ref.at[:, columns(rel ^ d)], t.at[rel], sem_t.at[rel])
            for rel in range(16)
        ]
        first = pltpu.make_async_copy(ds_ref, ds, sem_one.at[0])

        def reads(j, parity):
            b = rel_of(j) ^ d
            factor = u_refs[4 * parity + j // 2 if isinstance(j, int) else 0]
            copies = [
                pltpu.make_async_copy(w_ref.at[b], w.at[j], sem_in.at[j, 0]),
                pltpu.make_async_copy(ct_ref.at[:, columns(b)], ct.at[j], sem_in.at[j, 1]),
                pltpu.make_async_copy(factor.at[1, half], u.at[j], sem_in.at[j, 2]),
                pltpu.make_async_copy(r5_ref.at[:, spot(j)], r.at[j, 0], sem_r.at[j, 0]),
            ]
            for p in range(pieces):
                for i, refs in ((1, r6_refs), (2, r7_refs)):
                    copies.append(
                        pltpu.make_async_copy(
                            refs[p].at[:, spot(j)],
                            r.at[j, i, pl.ds(p * height, height)],
                            sem_r.at[j, 1 + 2 * p + i - 1],
                        )
                    )
            return copies

        def writes(j, parity):
            b = rel_of(j) ^ d
            pairs = [(outs.at[j], out_ref.at[:, columns(b)]), (gs.at[j], g_ref.at[:, spot(j)])]
            for i, ref in enumerate((o5_ref, o6_ref, o7_ref)):
                pairs.append((gone.at[j, i], ref.at[:, spot(j)]))
            if parity:
                pairs.append((gs.at[j], x_ref.at[j // 2]))
            return [pltpu.make_async_copy(a, c, sem_out.at[j, i]) for i, (a, c) in enumerate(pairs)]

        first.start()
        start_all(token_reads)
        for j in range(8):
            start_all(reads(j, j % 2))
        first.wait()
        wait_all(token_reads)

        def group(base, carry):
            js = [4 * base + i for i in range(4)]
            for i, j in enumerate(js):
                wait_all(reads(j, i % 2))
            live = lax.broadcasted_iota(jnp.int32, (rows, BLK), 0) < alive
            scale = 0.7978845608028654
            for i, j in enumerate(js):
                within = 4 * (i // 2) + 2 * half + i % 2
                fed = [t[8 * (base ^ (k // 8)) + (within ^ (k % 8))] for k, _ in LOCAL]
                fed += [r[j, n] for n in range(3)]
                hidden = dot(jnp.concatenate(fed, 1), w[j].reshape(8 * BLK, BLK))
                hidden += dot_nt(ds[...], u[j])
                square = hidden * hidden
                bent = jnp.tanh(scale * hidden * (1.0 + 0.044715 * square))
                up = 0.5 * (1.0 + bent)
                slope = up + 0.5 * hidden * (1.0 - bent * bent) * scale * (1.0 + 0.134145 * square)
                outs[j] = jnp.where(live, hidden * up, 0.0).astype(BF16)
                gs[j] = jnp.where(live, ct[j].astype(F32) * slope, 0.0).astype(BF16)
            for j in js:
                back = dot_nt(gs[j], w[j, 5:8].reshape(3 * BLK, BLK)).astype(BF16)
                for i in range(3):
                    gone[j, i] = back[:, i * BLK : (i + 1) * BLK]
            grads = jnp.concatenate([gs[j] for j in js], 1)
            factors = jnp.concatenate([u[j] for j in js], 0)
            part[...] = jnp.where(base == 0, 0.0, part[...]) + dot(grads, factors)
            for i, j in enumerate(js):
                start_all(writes(j, i % 2))
            return carry

        part[...] = jnp.zeros_like(part)
        lax.fori_loop(0, 2, group, 0)
        sent = []
        for j in range(8):
            sent += writes(j, j % 2)
        last = pltpu.make_async_copy(part, up_ref, sem_one.at[1])
        last.start()
        wait_all(sent)
        last.wait()

    operands = [tokens, far[0], *far[1], *far[2], weights, down_sum, *up_own, *up_mate, cotangent]
    aliases = {}
    if carried is not None:
        aliases = {len(operands) + 1: 0}
        operands.append(carried)
    blocks = pltpu.VMEM((8, rows, BLK), BF16)
    scratch = [
        pltpu.VMEM((16, rows, BLK), BF16),
        pltpu.VMEM((8, 3, rows, BLK), BF16),
        pltpu.VMEM((8, 8, BLK, BLK), BF16),
        pltpu.VMEM((rows, BLK), BF16),
        blocks,
        blocks,
        blocks,
        blocks,
        pltpu.VMEM((8, 3, rows, BLK), BF16),
        pltpu.VMEM((rows, BLK), F32),
        pltpu.SemaphoreType.DMA((16,)),
        pltpu.SemaphoreType.DMA((8, 5)),
        pltpu.SemaphoreType.DMA((8, 3)),
        pltpu.SemaphoreType.DMA((8, 9)),
        pltpu.SemaphoreType.DMA((2,)),
    ]
    out_shape = [struct(rows, 4096)] + [struct(rows, 2048)] * 4
    out_shape += [struct(4, rows, BLK), struct(rows, BLK, dtype=F32)]
    return local_call(
        body, info, operands, out_shape, scratch, 8 * 13 * 2 * rows * BLK * BLK, 22 << 20, aliases
    )


def grads_of(info, half, groups, tokens, mate_tokens, far, mate_far, grad, packed, sums):
    rows = tokens.shape[0]
    pieces = len(far[1])
    jobs, sizes = [], []
    for number, group in enumerate(groups):
        at = 0
        for xr, low, high in group:
            for m in range(low, high):
                jobs.append((number, at, xr, m))
                at += 1
        sizes.append(at)
    used = []
    for _, _, xr, _ in jobs:
        if xr not in used:
            used.append(xr)

    def body(s_ref, t_ref, tm_ref, *rest):
        remote = []
        for i in range(2):
            flat = rest[i * (1 + 2 * pieces) : (i + 1) * (1 + 2 * pieces)]
            remote.append((flat[:1], flat[1 : 1 + pieces], flat[1 + pieces :]))
        rest = rest[2 * (1 + 2 * pieces) :]
        g_ref, x_ref, da_ref, db_ref = rest[:4]
        out_refs = rest[4 : 4 + len(sizes)]
        feed, held, outs, sem_f, sem_h, sem_out = rest[-6:]
        d = s_ref[0]

        def block(xr):
            return (4 * xr + 2 * half) ^ d

        top, bottom = pl.ds(0, rows), pl.ds(rows, rows)

        def grad_pairs(xr, to):
            return [
                (g_ref.at[:, columns(place(block(xr)))], to.at[top]),
                (x_ref.at[xr], to.at[bottom]),
            ]

        shared = []
        for i, xr in enumerate(used):
            for n, (source, to) in enumerate(grad_pairs(xr, held.at[i])):
                shared.append(pltpu.make_async_copy(source, to, sem_h.at[i, n]))
        for n, (source, where) in enumerate(((da_ref, top), (db_ref, bottom))):
            shared.append(
                pltpu.make_async_copy(source, held.at[len(used), where], sem_h.at[len(used), n])
            )

        def reads(n):
            _, _, xr, m = jobs[n]
            if m == 8:
                pairs = grad_pairs(xr, feed.at[n])
            elif m < 5:
                p = columns(block(xr) ^ LOCAL[m][0])
                pairs = [(t_ref.at[:, p], feed.at[n, top]), (tm_ref.at[:, p], feed.at[n, bottom])]
            else:
                p = columns(place(block(xr)))
                pairs = []
                for i in range(2):
                    refs = remote[i][m - 5]
                    tall = rows // len(refs)
                    for q, ref in enumerate(refs):
                        pairs.append((ref.at[:, p], feed.at[n, pl.ds(i * rows + q * tall, tall)]))
            return [pltpu.make_async_copy(a, c, sem_f.at[n]) for a, c in pairs]

        start_all(shared)
        for n in range(len(jobs)):
            start_all(reads(n))
        wait_all(shared)
        slots = [len(used) if m == 8 else used.index(xr) for _, _, xr, m in jobs]
        cut = len(jobs) // 4

        def part(i, carry):
            for q in range(cut):
                whole = feed.at[cut * i + q]
                pltpu.make_async_copy(whole, whole, sem_f.at[cut * i + q]).wait()
            for q in range(cut):
                slot = jnp.where(
                    i < 2,
                    jnp.where(i == 0, slots[q], slots[cut + q]),
                    jnp.where(i == 2, slots[2 * cut + q], slots[3 * cut + q]),
                )
                outs[cut * i + q] = dot_tn(feed[cut * i + q], held[slot]).astype(BF16)
            return carry

        lax.fori_loop(0, 4, part, 0)
        sent = []
        for n, (number, at, _, _) in enumerate(jobs):
            sent.append(pltpu.make_async_copy(outs.at[n], out_refs[number].at[at], sem_out.at[n]))
        start_all(sent)
        wait_all(sent)

    count = len(jobs)
    scratch = [
        pltpu.VMEM((count, 2 * rows, BLK), BF16),
        pltpu.VMEM((len(used) + 1, 2 * rows, BLK), BF16),
        pltpu.VMEM((count, BLK, BLK), BF16),
        pltpu.SemaphoreType.DMA((count,)),
        pltpu.SemaphoreType.DMA((len(used) + 1, 2)),
        pltpu.SemaphoreType.DMA((count,)),
    ]
    return local_call(
        body, info,
        [tokens, mate_tokens, far[0], *far[1], *far[2], mate_far[0], *mate_far[1], *mate_far[2],
         grad, packed, *sums],
        [struct(size, BLK, BLK) for size in sizes], scratch,
        count * 4 * rows * BLK * BLK, count * 3 * 2 * rows * BLK,
    )


def down_grads(info, tokens, mate_tokens, ups):
    rows = tokens.shape[0]

    def body(s_ref, t_ref, tm_ref, ua_ref, ub_ref, *rest):
        out_refs = rest[:4]
        feed, up, outs, sem_f, sem_u, sem_out = rest[4:]
        d = s_ref[0]
        top, bottom = pl.ds(0, rows), pl.ds(rows, rows)
        shared = [
            pltpu.make_async_copy(ua_ref, up.at[top], sem_u.at[0]),
            pltpu.make_async_copy(ub_ref, up.at[bottom], sem_u.at[1]),
        ]

        def reads(n):
            p = columns((2 * n) ^ d)
            return [
                pltpu.make_async_copy(t_ref.at[:, p], feed.at[n, top], sem_f.at[n, 0]),
                pltpu.make_async_copy(tm_ref.at[:, p], feed.at[n, bottom], sem_f.at[n, 1]),
            ]

        start_all(shared)
        for n in range(8):
            start_all(reads(n))
        wait_all(shared)
        sent = []
        for n in range(8):
            wait_all(reads(n))

        def group(base, carry):
            for i in range(4):
                outs[4 * base + i] = dot_tn(feed[4 * base + i], up[...]).astype(BF16)
            return carry

        lax.fori_loop(0, 2, group, 0)
        for n in range(8):
            copy = pltpu.make_async_copy(outs.at[n], out_refs[n // 2].at[n % 2], sem_out.at[n])
            copy.start()
            sent.append(copy)
        wait_all(sent)

    scratch = [
        pltpu.VMEM((8, 2 * rows, BLK), BF16),
        pltpu.VMEM((2 * rows, BLK), BF16),
        pltpu.VMEM((8, BLK, BLK), BF16),
        pltpu.SemaphoreType.DMA((8, 2)),
        pltpu.SemaphoreType.DMA((2,)),
        pltpu.SemaphoreType.DMA((8,)),
    ]
    return local_call(
        body, info, [tokens, mate_tokens, *ups], [struct(2, BLK, BLK)] * 4, scratch,
        8 * 4 * rows * BLK * BLK, 5 << 20,
    )


def back_all(info, grads, weights, up_sum, down_own, down_mate, from_y, from_z):
    rows = grads[0].shape[0]

    def body(s_ref, g0_ref, g1_ref, w_ref, us_ref, *rest):
        d_refs, (y0, y1, z0, z1, out_ref) = rest[:8], rest[8:13]
        g, w, us, dn, ys, zs, outs, sem_in, sem_out, sem_one = rest[13:]
        d = s_ref[0]
        first = pltpu.make_async_copy(us_ref, us, sem_one.at[0])

        def reads(rel):
            half, p = (rel // 2) % 2, columns(place(rel ^ d))
            return [
                pltpu.make_async_copy((g0_ref, g1_ref)[half].at[:, p], g.at[rel], sem_in.at[rel, 0]),
                pltpu.make_async_copy(
                    w_ref.at[rel ^ d, pl.ds(0, 5)], w.at[rel], sem_in.at[rel, 1]
                ),
            ]

        def extras(rel):
            half, p = (rel // 2) % 2, columns(place(rel ^ d))
            return [
                pltpu.make_async_copy(
                    d_refs[4 * (rel % 2) + rel // 4].at[0, (rel // 2) % 2],
                    dn.at[rel],
                    sem_in.at[rel, 2],
                ),
                pltpu.make_async_copy((y0, y1)[half].at[:, p], ys.at[rel], sem_in.at[rel, 3]),
                pltpu.make_async_copy((z0, z1)[half].at[:, p], zs.at[rel], sem_in.at[rel, 4]),
            ]

        first.start()
        for rel in range(16):
            start_all(reads(rel))
            start_all(extras(rel))
        first.wait()
        for rel in range(16):
            wait_all(reads(rel))
            wait_all(extras(rel))

        def write(rel):
            return pltpu.make_async_copy(
                outs.at[rel], out_ref.at[:, columns(rel ^ d)], sem_out.at[rel]
            )

        def group(xr, carry):
            for low in range(4):
                others = [4 * (xr ^ (k // 4)) + (low ^ (k % 4)) for k, _ in LOCAL]
                rel = 4 * xr + low
                fed = jnp.concatenate([g[o] for o in others] + [us[...]], 1)
                rhs = [w[o, level] for o, (_, level) in zip(others, LOCAL)] + [dn[rel]]
                total = dot_nt(fed, jnp.concatenate(rhs, 1))
                total += ys[rel].astype(F32) + zs[rel].astype(F32)
                outs[rel] = total.astype(BF16)
            for low in range(4):
                write(4 * xr + low).start()
            return carry

        lax.fori_loop(0, 4, group, 0)
        for rel in range(16):
            write(rel).wait()

    operands = [*grads, weights, up_sum, *down_own, *down_mate, *from_y, *from_z]
    blocks = pltpu.VMEM((16, rows, BLK), BF16)
    scratch = [
        blocks,
        pltpu.VMEM((16, 5, BLK, BLK), BF16),
        pltpu.VMEM((rows, BLK), BF16),
        blocks,
        blocks,
        blocks,
        blocks,
        pltpu.SemaphoreType.DMA((16, 5)),
        pltpu.SemaphoreType.DMA((16,)),
        pltpu.SemaphoreType.DMA((1,)),
    ]
    return local_call(
        body, info, operands, [struct(rows, 4096)], scratch, 16 * 6 * 2 * rows * BLK * BLK, 22 << 20
    )[0]


def after(values, other):
    return lax.optimization_barrier((tuple(values), other))[0]


def gather_factors(down, up):
    both = jnp.stack([down, up])
    pair = jnp.stack([both, send(both, Y1)], 1)
    own = [pair] + [send(pair, move) for move in (X1, X2, X3)]
    return own, [send(piece, CORE) for piece in own]


def sum_over_mp(part):
    def both(a, b):
        return a.astype(F32) + b.astype(F32)

    pair = both(part, send(part, Y2)).astype(BF16)
    moved = [send(pair, move) for move in (Z1, Z2, Z3)]
    return (both(pair, moved[0]) + both(moved[1], moved[2])).astype(BF16)


def program(tokens, block_weights, lowrank_down, lowrank_up, cotangent, seq_lengths):
    me = lax.axis_index("dp").astype(jnp.int32)
    info = jnp.stack([me, seq_lengths[0]])

    whole_a, low_rows, high_rows, whole_b = take_halves(info, tokens)

    def exchange(whole, parts):
        r6 = [send(part, Z1) for part in parts]
        r7 = [send(part, Z3) for part in r6]
        return send(whole, Y2), r6, r7

    far_a = exchange(whole_a, [low_rows, high_rows])
    far_b = exchange(whole_b, [whole_b])
    factors_own, factors_mate = gather_factors(lowrank_down, lowrank_up)
    mate_tokens = send(tokens, CORE)
    part = down_part(info, tokens, factors_own, factors_mate)
    down_sum = sum_over_mp(part)
    mate_down = send(down_sum, CORE)
    sums = (down_sum, mate_down)

    def to_mate(far):
        return (
            send(far[0], CORE), [send(v, CORE) for v in far[1]], [send(v, CORE) for v in far[2]]
        )

    mate_a, mate_b = to_mate(far_a), to_mate(far_b)

    def forward(half, far, carried):
        output, grad, t5, t6, t7, pack, up = forward_half(
            info, half, tokens, far, block_weights, down_sum, factors_own, factors_mate,
            cotangent, carried,
        )
        pack = send(pack, CORE)
        return output, grad, (t5, t6, t7), pack, up

    def terms_back(terms, other):
        carried = send(terms[2], Z3)
        from_y = send(terms[0], Y2)
        carried = after((carried,), other)[0]
        joined = (terms[1].astype(F32) + carried.astype(F32)).astype(BF16)
        return from_y, send(joined, Z1)

    def local_grads(half, far, mate_far, grad, pack):
        fixed = (tokens, mate_tokens, far, mate_far, grad, pack, sums)
        groups = (((2, 0, 5), (1, 0, 5)), ((2, 5, 9), (3, 5, 9)), ((1, 5, 9),), ((3, 0, 5),))
        groups += (((0, 0, 5),), ((0, 5, 9),))
        made = grads_of(info, half, groups, *fixed)
        return made[:2], made[2:]

    def over_x(gone, rest, extra, other):
        to1, to3 = gone
        late1, late3, own_low, own_high = rest
        got1 = send(to1, X1)
        got3 = send(to3, X3)
        got1, got3 = after((got1, got3), other)
        late1 = (late1.astype(F32) + got3[:4].astype(F32)).astype(BF16)
        late3 = (late3.astype(F32) + got1[:5].astype(F32)).astype(BF16)
        if extra:
            late1 = jnp.concatenate([late1, extra[0]])
            late3 = jnp.concatenate([late3, extra[1]])
        end1 = send(late1, X1)
        end3 = send(late3, X3)
        return (got1, got3, end1, end3, own_low, own_high), late3

    def finish(parts, other):
        got1, got3, end1, end3, own_low, own_high = parts
        end1, end3 = after((end1, end3), other)
        low = own_low.astype(F32) + got1[5:].astype(F32) + end3[:5].astype(F32)
        high = own_high.astype(F32) + got3[4:].astype(F32) + end1[:4].astype(F32)
        return low, high

    output, grad_a, terms_a, pack_a, up_a = forward(1, far_a, None)
    gone_a, rest_a = local_grads(1, far_a, mate_a, grad_a, pack_a)

    output, grad_b, terms_b, pack_b, up_b = forward(0, far_b, output)
    x_a, late_a = over_x(gone_a, rest_a, None, up_b)
    y_a, z_a = terms_back(terms_a, late_a)
    gone_b, rest_b = local_grads(0, far_b, mate_b, grad_b, pack_b)
    y_b, z_b = terms_back(terms_b, rest_b[0])
    low_a, high_a = finish(x_a, rest_b[0])
    across = send(jnp.concatenate([low_a, high_a]).astype(BF16), Y1)

    up_sum = sum_over_mp((up_a + up_b).astype(BF16))
    mate_up = send(up_sum, CORE)
    d0, d1, d2, d3 = down_grads(info, tokens, mate_tokens, (up_sum, mate_up))
    d2 = send(d2, X2)
    x_b, _ = over_x(gone_b, rest_b, (d1, d3), d0)
    grad_tokens = back_all(
        info, (grad_b, grad_a), block_weights, up_sum, factors_own, factors_mate,
        (y_b, y_a), (z_b, z_a),
    )
    end1, end3, d2 = after((x_b[2], x_b[3], d2), grad_tokens)
    x_b = x_b[:2] + (end1, end3) + x_b[4:]
    d1, d3 = end1[4:], end3[5:]
    downs = d0.astype(F32) + d1.astype(F32) + d2.astype(F32) + d3.astype(F32)
    sent_down = downs[1].astype(BF16)
    grad_down = (downs[0] + send(sent_down, Y1).astype(F32)).astype(BF16)
    low_b, high_b = finish(x_b, sent_down)
    across = after((across,), sent_down)[0]
    grad_low = low_b + across[:5].astype(F32)
    grad_high = high_b + across[5:].astype(F32)
    grad_blocks = jnp.concatenate([grad_low, grad_high[:3]]).astype(BF16)[None]
    grad_lowrank = jnp.stack([grad_down, grad_high[3].astype(BF16)], 1)
    return (output, grad_tokens, grad_blocks, grad_lowrank)


def solution(mesh):
    placed = (
        P("dp", "mp"),
        P("mp", None, None, None),
        P(("mp", "dp"), None),
        P(("mp", "dp"), None),
        P("dp", "mp"),
        P("dp"),
    )
    return jax.shard_map(
        program,
        mesh=mesh,
        in_specs=placed,
        out_specs=(
            P("dp", "mp"),
            P("dp", "mp"),
            P(("mp", "dp"), None, None, None),
            P(("mp", "dp"), None, None),
        ),
        check_vma=False,
    )
```
